512 devices in a mesh: section: 16 (over y, core), expert: 32 (over x, z).
Axes of the slice: x: 4, y: 8, z: 8, core: 2. Of those that a mesh axis runs over, the one named last changes fastest.
Arguments:
- saved_inputs: bfloat16 [16, 2, 256, 2048], P('section', None, 'expert'), may hold values from -6 to 6
- top_grad: bfloat16 [2, 256, 2048], P(None, 'expert'), may hold values from -6 to 6
- expert_ids: int32 [16, 2, 256, 2], P('section', None, 'expert'), may hold values from 0 to 7, all different within a row; in each aligned block of 8 rows (0 to 7, 8 to 15, ..., all dimensions but the last counted through in order) at most 3 rows name the same one
- route_weights: bfloat16 [16, 2, 256, 2], P('section', None, 'expert'), may hold values from 0.099609375 to 0.59765625
- example_ids: int32 [2, 256], P(None, 'expert'), may hold values from 0 to 3, never falling along the last dimension, each value on 1 to 128 neighbouring positions
- gate_weight: bfloat16 [16, 12288, 2048], P('section', 'expert'), may hold values from -0.125 to 0.125
- up_weight: bfloat16 [16, 12288, 2048], P('section', 'expert'), may hold values from -0.125 to 0.125
- down_weight: bfloat16 [16, 12288, 2048], P('section', 'expert'), may hold values from -0.15625 to 0.15625
- left_proj: bfloat16 [16, 12288, 64], P('section', 'expert'), may hold values from -0.15625 to 0.15625
- right_proj: bfloat16 [16, 2048, 64], P('section'), may hold values from -0.125 to 0.125
Outputs:
- input_grads: bfloat16 [16, 2, 256, 2048], P('section', None, 'expert')
- sketches: float32 [16, 64, 4096], P('section', 'expert')
The draws below stay inside these ranges and needn't reach their ends.
Inputs may be any that keep to these rules, and one draw needn't show every extreme that they name: `expert_ids`: each row names 2 different experts; in each aligned block of 8 rows (one device's tokens of one layer and micro-batch) no expert is named by more than 3 rows, and some block reaches 3. `example_ids`: along each micro-batch the example number never falls and every example has a token.
All inputs are finite; a program needn't handle non-finite values.
Results may differ from the reference program's by a relative error of at most 0.028.
Values may be sent and summed in bfloat16 or wider, within the bound.
A program may use at most 64 MiB of HBM per device.

```python
import math
import jax
import jax.numpy as jnp
import numpy as np
from jax import lax

D = 2048
FF = 1536
EXPERTS = 8
TOPK = 2
R = 64
MICRO = 2
EXM = 4
TOK_DEV = 8
CAP = 3
LAYERS = 16
TOKENS = 256
N_EXPERT = 32


def shard_levels(key, dims, cuts, least, high):
    def one(axis_at, shards_of):
        steps = jax.random.uniform(jax.random.fold_in(jax.random.fold_in(key, 6), axis_at), (shards_of,), jnp.float32, least / len(cuts), high / len(cuts))
        return jnp.repeat(jnp.exp(steps), dims[axis_at] // shards_of).reshape((-1,) + (1,) * (len(dims) - axis_at - 1))

    loudness = one(*cuts[0])
    for cut in cuts[1:]:
        loudness = loudness * one(*cut)
    return loudness


def length_profile(amount, total, limit, lean):
    weights = [(1 << 20) // math.isqrt(grade ** lean) + 1 for grade in range(2, amount + 1)]
    spare, counts = total - limit - (amount - 1), [1] * (amount - 1)
    while spare > 0:
        free = [i for i in range(amount - 1) if counts[i] < limit]
        whole, remaining = sum([weights[i] for i in free]), spare
        for i in free:
            extra = min(limit - counts[i], max(1, remaining * weights[i] // whole), spare)
            counts[i] = counts[i] + extra
            spare = spare - extra
    return np.array([limit] + counts)


def ragged_sizes(rng, amount, total, limit, skew):
    if amount == 2:
        one = jax.random.randint(rng, (), max(1, total - limit), min(limit, total - 1) + 1)
        return jnp.stack([one, total - one])
    tallies = jnp.asarray(length_profile(amount, total, limit, skew), jnp.int32)
    pairs = (amount - 1) // 2
    donor, taker = tallies[1:1 + 2 * pairs:2], tallies[2:2 + 2 * pairs:2]
    slack = jnp.minimum(donor - 1, limit - taker)
    shifted = jax.random.randint(jax.random.fold_in(rng, 1), (pairs,), 0, 1 << 20) % (slack + 1)
    tallies = tallies.at[1:1 + 2 * pairs:2].set(donor - shifted).at[2:2 + 2 * pairs:2].set(taker + shifted)
    return tallies[jax.random.permutation(jax.random.fold_in(rng, 2), amount)]


def shared_out(rng, own, number, rows, count, top, limit, lean):
    ranking = jax.random.permutation(rng, count)
    heavy_load, common = shares(count, rows * top, limit, lean, True), shares(count, rows * top, limit, lean, False)
    places = jnp.arange(count)

    def named(sizes, turn):
        used = int((sizes > 0).sum())
        fixed = max(1, used // 4)
        shifted = fixed + (places - fixed + turn * (used - fixed)) % max(1, count - fixed)
        return jnp.zeros((count,), jnp.int32).at[ranking[jnp.where(places < fixed, places, shifted)]].set(jnp.asarray(sizes, jnp.int32))

    sizes = jnp.where(number % 4 == 0, named(heavy_load, number // 4), named(common, number - number // 4 - 1))
    mixed = jax.random.permutation(jax.random.fold_in(own, 3), count)
    giver, receiver = mixed[0:count // 2 * 2:2], mixed[1:count // 2 * 2:2]
    slack = jnp.minimum(sizes[giver] - 1, limit - sizes[receiver]) // 2
    slack = jnp.where((giver == ranking[0]) | (receiver == ranking[0]) | (sizes[receiver] == 0), 0, jnp.maximum(slack, 0))
    shifted = jax.random.randint(jax.random.fold_in(own, 4), (count // 2,), 0, 1 << 20) % (slack + 1)
    sizes = sizes.at[giver].add(-shifted).at[receiver].add(shifted)
    members = jnp.searchsorted(jnp.cumsum(sizes), jnp.arange(rows * top), side="right").astype(jnp.int32)
    table = members.reshape(top, rows).T
    table = table[jax.random.permutation(jax.random.fold_in(own, 1), rows)]
    turn = jax.random.randint(jax.random.fold_in(own, 2), (rows, 1), 0, top)
    return jnp.take_along_axis(table, (jnp.arange(top)[None, :] + turn) % top, axis=1)


def shares(number_of, total, limit, lean, full):
    weights = [(1 << 20) // math.isqrt(standing ** lean) + 1 for standing in range(1, number_of + 1)]
    largest = limit if full else min(limit, max(-(-total // number_of), total * weights[0] // sum(weights)))
    least = 1 if total - largest >= number_of - 1 else 0
    counts, surplus = [largest] + [least] * (number_of - 1), total - largest - least * (number_of - 1)
    while surplus > 0:
        free = [i for i in range(1, number_of) if counts[i] < largest] or [i for i in range(1, number_of) if counts[i] < limit]
        pool, left = sum([weights[i] for i in free]), surplus
        for i in free:
            addition = min(limit - counts[i], max(1, left * weights[i] // pool), surplus)
            counts[i] = counts[i] + addition
            surplus = surplus - addition
    return np.array(counts)


def scatter_about(own_key, dims, scale, bound, split=(), kind=jnp.bfloat16):
    entries = scale * jax.random.normal(own_key, dims, jnp.float32)
    if split:
        entries = entries * shard_levels(own_key, dims, split, -0.22, 0.18)
    return jnp.clip(entries, -bound, bound).astype(kind)


def setup_inputs(seed: int = 0) -> dict:
    splits = jax.random.split(jax.random.key(seed), 11)
    saved_inputs = scatter_about(splits[0], (LAYERS, MICRO, TOKENS, D), 1.0, 6.0, ((0, 16), (2, 32)))
    top_grad = scatter_about(splits[1], (MICRO, TOKENS, D), 1.0, 6.0, ((1, 32),))
    expert_ids_keys = jax.random.split(jax.random.fold_in(splits[2], 1), LAYERS * MICRO * TOKENS // TOK_DEV)
    expert_ids_turns = jax.random.permutation(jax.random.fold_in(splits[2], 3), LAYERS * MICRO * TOKENS // TOK_DEV)
    expert_ids = jax.vmap(lambda own, number: shared_out(jax.random.fold_in(splits[2], 2), own, number, TOK_DEV, EXPERTS, TOPK, CAP, 2))(expert_ids_keys, expert_ids_turns).reshape((LAYERS, MICRO, TOKENS, TOPK))
    route_weights = jnp.clip(0.099609375 + 0.49804688 * jax.random.uniform(splits[3], (LAYERS, MICRO, TOKENS, TOPK), jnp.float32) ** shard_levels(splits[3], (LAYERS, MICRO, TOKENS, TOPK), ((0, 16), (2, 32)), -0.2, 0.2), 0.099609375, 0.59765625).astype(jnp.bfloat16)
    example_ids = jax.vmap(lambda own: jnp.searchsorted(jnp.cumsum(ragged_sizes(own, EXM, TOKENS, TOKENS // 2, 1)), jnp.arange(TOKENS), side="right"))(jax.random.split(splits[4], MICRO)).reshape((MICRO, TOKENS)).astype(jnp.int32)
    gate_weight = scatter_about(splits[5], (LAYERS, EXPERTS * FF, D), D ** -0.5, 0.125, ((0, 16), (1, 32)))
    up_weight = scatter_about(splits[6], (LAYERS, EXPERTS * FF, D), D ** -0.5, 0.125, ((0, 16), (1, 32)))
    down_weight = scatter_about(splits[7], (LAYERS, EXPERTS * FF, D), FF ** -0.5, 0.15625, ((0, 16), (1, 32)))
    left_proj = scatter_about(splits[8], (LAYERS, EXPERTS * FF, R), FF ** -0.5, 0.15625, ((0, 16), (1, 32)))
    right_proj = scatter_about(splits[9], (LAYERS, D, R), D ** -0.5, 0.125, ((0, 16),))
    return dict(saved_inputs=saved_inputs, top_grad=top_grad, expert_ids=expert_ids, route_weights=route_weights, example_ids=example_ids, gate_weight=gate_weight, up_weight=up_weight, down_weight=down_weight, left_proj=left_proj, right_proj=right_proj)


def reference(saved_inputs, top_grad, expert_ids, route_weights, example_ids, gate_weight, up_weight, down_weight, left_proj, right_proj):
    hsplit = N_EXPERT // EXPERTS
    group = FF // hsplit
    q_total = MICRO * EXM * EXPERTS

    def one_layer(out_grads, packed):
        inputs, route_ids, route_w, w_gate, w_up, w_down, proj_left, proj_right = packed
        w_gate = w_gate.reshape(EXPERTS, FF, D)
        w_up = w_up.reshape(EXPERTS, FF, D)
        w_down = w_down.reshape(EXPERTS, FF, D)
        proj_left = proj_left.reshape(EXPERTS, FF, R)
        new_list = []
        sketch = jnp.zeros((q_total * R, R), jnp.float32)
        for m in range(MICRO):
            acts = inputs[m]
            out_grad = out_grads[m]
            summed_grad = out_grad.astype(jnp.float32)
            right_tok = jnp.dot(out_grad, proj_right, preferred_element_type=jnp.float32)
            for e in range(EXPERTS):
                route = jnp.sum(jnp.where(route_ids[m] == e, route_w[m].astype(jnp.float32), jnp.float32(0.0)), axis=1)
                pre_gate = jnp.dot(acts, w_gate[e].T, preferred_element_type=jnp.float32)
                pre_up = jnp.dot(acts, w_up[e].T, preferred_element_type=jnp.float32)
                sigmoid_g = jax.nn.sigmoid(pre_gate)
                hidden = (pre_gate * sigmoid_g * pre_up).astype(jnp.bfloat16)
                left_part = jnp.einsum("tjh,jhr->tjr", hidden.reshape(TOKENS, hsplit, group).astype(jnp.float32),
                                       proj_left[e].reshape(hsplit, group, R).astype(jnp.float32))
                left_part = lax.optimization_barrier(left_part.astype(jnp.bfloat16))
                left_factor = jnp.sum(left_part.astype(jnp.float32), axis=1)
                grad_hidden = jnp.dot(out_grad, w_down[e].T, preferred_element_type=jnp.float32) * route[:, None]
                grad_gate = (grad_hidden * pre_up * sigmoid_g * (1.0 + pre_gate * (1.0 - sigmoid_g))).astype(jnp.bfloat16)
                grad_up = (grad_hidden * pre_gate * sigmoid_g).astype(jnp.bfloat16)
                part_grad = jnp.einsum("tjh,jhd->tjd", grad_gate.reshape(TOKENS, hsplit, group).astype(jnp.float32),
                                       w_gate[e].reshape(hsplit, group, D).astype(jnp.float32))
                part_grad = part_grad + jnp.einsum("tjh,jhd->tjd", grad_up.reshape(TOKENS, hsplit, group).astype(jnp.float32),
                                                   w_up[e].reshape(hsplit, group, D).astype(jnp.float32))
                part_grad = lax.optimization_barrier(part_grad.astype(jnp.bfloat16))
                summed_grad = summed_grad + jnp.sum(part_grad.astype(jnp.float32), axis=1)
                right_factor = right_tok * route[:, None]
                query = (m * EXM + example_ids[m]) * EXPERTS + e
                query_hot = (query[:, None] == jnp.arange(q_total, dtype=jnp.int32)[None, :]).astype(jnp.float32)
                outer_rows = (query_hot[:, :, None] * left_factor[:, None, :]).reshape(TOKENS, q_total * R)
                sketch = sketch + jnp.dot(outer_rows.T, right_factor, precision=lax.Precision.HIGHEST)
            new_list.append(summed_grad.astype(jnp.bfloat16))
        new_grads = jnp.stack(new_list)
        return new_grads, (new_grads, sketch.reshape(q_total, R * R))

    packed_all = (saved_inputs, expert_ids, route_weights, gate_weight, up_weight, down_weight, left_proj, right_proj)
    final_grads, outputs = lax.scan(one_layer, top_grad, packed_all, reverse=True)
    return outputs[0], outputs[1]
```

```python
import functools

import jax
import jax.numpy as jnp
from jax import lax
from jax.experimental import pallas as pl
from jax.experimental.pallas import tpu as pltpu
from jax.sharding import PartitionSpec as P

EXPERTS = 8
EXM = 4
CAP = 3
LANES = 128
F32 = jnp.float32
BF16 = jnp.bfloat16
MESH = pl.DeviceIdType.MESH


def kernel(
    n_section,
    n_expert,
    groups,
    tok_ref,
    row_ref,
    x_ref,
    top_ref,
    meta_ref,
    left_ref,
    gate_hbm,
    up_hbm,
    down_hbm,
    right_hbm,
    grads_ref,
    sketch_ref,
    wgu,
    wdr,
    xsend,
    xrecv,
    gsend,
    grecv,
    osend,
    crecv_a,
    crecv_b,
    frecv_a,
    frecv_b,
    metar,
    outgrad,
    resid,
    back,
    wide,
    rows,
    gcat,
    coef_g,
    coef_u,
    left_keep,
    psend,
    srecv,
    w_sem,
    xs_sem,
    xr_sem,
    gs_sem,
    gr_sem,
    os_sem,
    cr_sem,
    fr_sem,
    ms_sem,
    mr_sem,
    rs_sem,
    rr_sem,
    bs_sem,
    br_sem,
    ss_sem,
    sr_sem,
):
    crecv, frecv = (crecv_a, crecv_b), (frecv_a, frecv_b)
    sec = lax.axis_index("section")
    me = lax.axis_index("expert")
    hsplit = n_expert // groups
    n_micro, tok_dev = top_ref.shape[:2]
    n_slots = groups * CAP
    dk = x_ref.shape[1]
    hid = down_hbm.shape[0]
    top_k = row_ref.shape[0] // (n_micro * tok_dev)
    q_dev = n_micro * EXM * groups // n_expert
    r_dim = left_ref.shape[0]
    half = r_dim // 2
    last = sec == n_section - 1
    first = sec == 0

    loads = [
        pltpu.make_async_copy(gate_hbm, wgu.at[pl.ds(0, hid)], w_sem.at[0]),
        pltpu.make_async_copy(up_hbm, wgu.at[pl.ds(hid, hid)], w_sem.at[1]),
        pltpu.make_async_copy(down_hbm, wdr.at[pl.ds(0, hid)], w_sem.at[2]),
        pltpu.make_async_copy(right_hbm, wdr.at[pl.ds(hid, r_dim)], w_sem.at[3]),
    ]
    for load in loads:
        load.start()

    barrier = pltpu.get_barrier_semaphore()

    def greet(other, skip_me):
        def one(n, carry):
            to = lax.rem(me + 1 + n, n_expert)
            pl.semaphore_signal(
                barrier, inc=1, device_id={"section": other, "expert": to}, device_id_type=MESH
            )
            return carry

        lax.fori_loop(0, n_expert - 1 if skip_me else n_expert, one, 0)

    greet(sec, True)

    @pl.when(jnp.logical_not(first))
    def _():
        greet(sec - 1, False)

    @pl.when(jnp.logical_not(last))
    def _():
        greet(sec + 1, False)

    def xbuild(m, carry):
        for s in range(n_slots):
            xsend[m, s] = x_ref[m * tok_dev + tok_ref[m * n_slots + s]]
        return carry

    lax.fori_loop(0, n_micro, xbuild, 0)

    met = (
        n_expert - 1
        + jnp.where(first, 0, n_expert)
        + jnp.where(last, 0, n_expert)
    )
    pl.semaphore_wait(barrier, met)

    def spread(src, per, dst, send_sem, recv_sem):
        def one(n, carry):
            to = lax.rem(me + 1 + n, n_expert)
            pltpu.make_async_remote_copy(
                src_ref=src.at[pl.ds((to // hsplit) * per, per)],
                dst_ref=dst.at[pl.ds(me * per, per)],
                send_sem=send_sem,
                recv_sem=recv_sem,
                device_id={"section": sec, "expert": to},
                device_id_type=MESH,
            ).start()
            return carry

        lax.fori_loop(0, n_expert - 1, one, 0)
        pltpu.make_async_copy(
            src.at[pl.ds((me // hsplit) * per, per)], dst.at[pl.ds(me * per, per)], recv_sem
        ).start()

    def await_all(ref, sem):
        pltpu.make_async_copy(ref, ref, sem).wait()

    def dispatch(m):
        for s in range(n_slots):
            gsend[m, s] = outgrad[m, tok_ref[m * n_slots + s]]
        spread(gsend.at[m], CAP, grecv.at[m], gs_sem.at[m], gr_sem.at[m])

        @pl.when(jnp.logical_not(first))
        def _():
            pltpu.make_async_remote_copy(
                src_ref=outgrad.at[m],
                dst_ref=resid.at[m],
                send_sem=rs_sem.at[m],
                recv_sem=rr_sem.at[m],
                device_id={"section": sec - 1, "expert": me},
                device_id_type=MESH,
            ).start()

        @pl.when(jnp.logical_not(last))
        def _():
            pltpu.make_async_remote_copy(
                src_ref=outgrad.at[m],
                dst_ref=back.at[m],
                send_sem=bs_sem.at[m],
                recv_sem=br_sem.at[m],
                device_id={"section": sec + 1, "expert": me},
                device_id_type=MESH,
            ).start()

    def combined(m, t, base, parts, which):
        total = base
        for k in range(top_k):
            at = row_ref[m * tok_dev * top_k + t * top_k + k, which]
            for j in range(hsplit):
                total = total + parts[at + j * CAP].astype(F32)
        return total

    def start_micro(m, carry):
        spread(xsend.at[m], CAP, xrecv.at[m], xs_sem.at[m], xr_sem.at[m])

        @pl.when(m == 0)
        def _():
            spread(meta_ref, 16, metar, ms_sem, mr_sem)

        @pl.when(last)
        def _():
            outgrad[m] = top_ref[m]
            dispatch(m)

        return carry

    lax.fori_loop(0, n_micro, start_micro, 0)

    def by_row(ref, m):
        wide[...] = ref[m].reshape(n_expert * CAP * dk, LANES).astype(F32)
        for k in range(dk):
            for c in range(CAP):
                rows[pl.ds(c * n_expert, n_expert), pl.ds(k * LANES, LANES)] = wide[
                    pl.ds(c * dk + k, n_expert, stride=CAP * dk), :
                ].astype(BF16)

    def meta_of(m):
        return jnp.concatenate(
            [
                jnp.concatenate(
                    [metar[pl.ds(b * 8 + m * 4 + c, n_expert, stride=16), :] for b in range(2)],
                    axis=1,
                )
                for c in range(CAP)
            ],
            axis=0,
        )

    contract_last = (((1,), (1,)), ((), ()))
    for load in loads:
        load.wait()
    await_all(metar, mr_sem)

    def forward(m, carry):
        await_all(xrecv.at[m], xr_sem.at[m])
        by_row(xrecv, m)
        both = lax.dot_general(rows[...], wgu[...], contract_last, preferred_element_type=F32)
        pre_gate, pre_up = both[:, :hid], both[:, hid:]
        sigmoid_g = jax.nn.sigmoid(pre_gate)
        silu = pre_gate * sigmoid_g
        hidden = (silu * pre_up).astype(BF16)
        left_keep[m] = lax.dot_general(
            hidden, left_ref[...], contract_last, preferred_element_type=F32
        )
        weight = jnp.max(meta_of(m), axis=1, keepdims=True)
        coef_g[m] = weight * (pre_up * sigmoid_g * (1.0 + pre_gate * (1.0 - sigmoid_g)))
        coef_u[m] = weight * silu
        return carry

    lax.fori_loop(0, n_micro, forward, 0)

    def to_homes(m, other, skip_me, dst, recv_sem):
        def one(n, carry):
            to = lax.rem(me + 1 + n, n_expert)
            pltpu.make_async_remote_copy(
                src_ref=osend.at[m, pl.ds(to * CAP, CAP)],
                dst_ref=dst.at[pl.ds(me * CAP, CAP)],
                send_sem=os_sem.at[m],
                recv_sem=recv_sem,
                device_id={"section": other, "expert": to},
                device_id_type=MESH,
            ).start()
            return carry

        lax.fori_loop(0, n_expert - 1 if skip_me else n_expert, one, 0)

    def sketch_copies(m):
        mine = me // hsplit
        copies = []
        for ex in range(EXM):
            q = (m * EXM + ex) * groups + mine
            to = q // q_dev
            src = psend.at[m, ex]
            dst = srecv.at[lax.rem(q, q_dev), lax.rem(me, hsplit)]
            far = pltpu.make_async_remote_copy(
                src_ref=src,
                dst_ref=dst,
                send_sem=ss_sem.at[m, ex],
                recv_sem=sr_sem,
                device_id={"section": sec, "expert": to},
                device_id_type=MESH,
            )
            near = pltpu.make_async_copy(src, dst, sr_sem)
            copies.append((to, far, near))
        return copies

    def step(m, carry):
        @pl.when(jnp.logical_not(last))
        def _():
            await_all(resid.at[m], rr_sem.at[m])
            for which in range(n_micro):

                @pl.when(m == which)
                def _():
                    await_all(crecv[which], cr_sem.at[which])
                    for t in range(tok_dev):
                        base = resid[which, t].astype(F32)
                        total = combined(which, t, base, crecv[which], 0)
                        outgrad[which, t] = total.astype(BF16)

            dispatch(m)

        await_all(grecv.at[m], gr_sem.at[m])
        by_row(grecv, m)
        both = lax.dot_general(
            rows[...], wdr[...], contract_last, preferred_element_type=F32
        )
        grad_hidden, right = both[:, :hid], both[:, hid:]
        gcat[:, pl.ds(0, hid)] = (grad_hidden * coef_g[m]).astype(BF16)
        gcat[:, pl.ds(hid, hid)] = (grad_hidden * coef_u[m]).astype(BF16)
        for n in range(dk // 2):
            part = jnp.dot(
                gcat[...], wgu[:, pl.ds(n * 2 * LANES, 2 * LANES)], preferred_element_type=F32
            )
            for b in range(2):
                k = n * 2 + b
                for c in range(CAP):
                    wide[pl.ds(c * dk + k, n_expert, stride=CAP * dk), :] = part[
                        c * n_expert : (c + 1) * n_expert, b * LANES : (b + 1) * LANES
                    ]
        osend[m] = wide[...].astype(BF16).reshape(n_expert * CAP, dk, LANES)

        for which in range(n_micro):

            @pl.when((m == which) & first)
            def _():
                to_homes(which, sec, True, frecv[which], fr_sem.at[which])
                pltpu.make_async_copy(
                    osend.at[which, pl.ds(me * CAP, CAP)],
                    frecv[which].at[pl.ds(me * CAP, CAP)],
                    fr_sem.at[which],
                ).start()

            @pl.when((m == which) & jnp.logical_not(first))
            def _():
                to_homes(which, sec - 1, False, crecv[which], cr_sem.at[which])

        right = jnp.concatenate([right] * EXM, axis=1) * meta_of(m)
        left = left_keep[m].astype(BF16)
        at_r = lax.broadcasted_iota(jnp.int32, (r_dim, r_dim), 0)
        at_c = lax.broadcasted_iota(jnp.int32, (r_dim, r_dim), 1)
        place = lax.rem(at_r, 2) * half + lax.div(at_r, 2)
        shuffle = jnp.where(at_c == place, 1.0, 0.0).astype(BF16)
        left = jnp.dot(left, shuffle, preferred_element_type=F32).astype(BF16)
        outer = lax.dot_general(
            left, right.astype(BF16), (((0,), (0,)), ((), ())), preferred_element_type=F32
        )
        for ex in range(EXM):
            block = outer[:, ex * r_dim : (ex + 1) * r_dim]
            psend[m, ex] = jnp.concatenate([block[:half], block[half:]], axis=1)
        for to, far, near in sketch_copies(m):

            @pl.when(to != me)
            def _():
                far.start()

            @pl.when(to == me)
            def _():
                near.start()

        return carry

    lax.fori_loop(0, n_micro, step, 0)

    @pl.when(first)
    def _():
        for m in range(n_micro):
            await_all(frecv[m], fr_sem.at[m])
            for t in range(tok_dev):
                total = combined(m, t, outgrad[m, t].astype(F32), frecv[m], 1)
                grads_ref[m, t] = total.astype(BF16)

    @pl.when(jnp.logical_not(first))
    def _():
        for m in range(n_micro):
            await_all(back.at[m], br_sem.at[m])
        grads_ref[...] = back[...]

    await_all(srecv, sr_sem)
    for q in range(q_dev):
        total = srecv[q, 0]
        for j in range(1, hsplit):
            total = total + srecv[q, j]
        sketch_ref[q] = total

    others = (n_expert - 1) * CAP
    await_all(metar.at[pl.ds(0, (n_expert - 1) * 16)], ms_sem)
    for m in range(n_micro):
        await_all(xrecv.at[m, pl.ds(0, others)], xs_sem.at[m])
        await_all(grecv.at[m, pl.ds(0, others)], gs_sem.at[m])

        @pl.when(first)
        def _():
            await_all(osend.at[m, pl.ds(0, others)], os_sem.at[m])

        @pl.when(jnp.logical_not(first))
        def _():
            await_all(osend.at[m], os_sem.at[m])
            await_all(outgrad.at[m], rs_sem.at[m])

        @pl.when(jnp.logical_not(last))
        def _():
            await_all(outgrad.at[m], bs_sem.at[m])

        for to, far, near in sketch_copies(m):

            @pl.when(to != me)
            def _():
                far.wait_send()


def on_device(
    saved_inputs,
    top_grad,
    expert_ids,
    route_weights,
    example_ids,
    gate_weight,
    up_weight,
    down_weight,
    left_proj,
    right_proj,
):
    n_section = lax.axis_size("section")
    n_expert = lax.axis_size("expert")
    groups = EXPERTS
    hsplit = n_expert // groups
    n_micro, tok_dev, feat = saved_inputs.shape[1:]
    top_k = expert_ids.shape[3]
    n_pairs = tok_dev * top_k
    n_slots = groups * CAP
    dk = feat // LANES
    hid = gate_weight.shape[1]
    r_dim = left_proj.shape[2]
    q_dev = n_micro * EXM * groups // n_expert

    ids = expert_ids[0].reshape(n_micro, n_pairs)
    weights = route_weights[0].reshape(n_micro, n_pairs).astype(F32)
    pair = jnp.arange(n_pairs, dtype=jnp.int32)
    same = (ids[:, :, None] == ids[:, None, :]) & (pair[:, None] > pair[None, :])[None]
    position = jnp.sum(same.astype(jnp.int32), axis=2)
    slot_of = ids * CAP + position
    row_of = ids * (hsplit * CAP) + position
    slots = jnp.arange(n_slots, dtype=jnp.int32)
    select = slot_of[:, None, :] == slots[None, :, None]
    tok_of_slot = jnp.sum(jnp.where(select, (pair // top_k)[None, None], 0), axis=2)
    slot_weight = jnp.sum(jnp.where(select, weights[:, None, :], 0.0), axis=2)
    example_pairs = jnp.repeat(example_ids, top_k, axis=1)
    slot_example = jnp.sum(jnp.where(select, example_pairs[:, None, :], 0), axis=2)
    lane_example = jnp.arange(EXM * r_dim, dtype=jnp.int32) // r_dim
    meta = jnp.where(
        slot_example[:, :, None] == lane_example[None, None], slot_weight[:, :, None], 0.0
    )
    meta = meta.reshape(n_micro, groups, CAP, EXM * r_dim).swapaxes(0, 1)
    meta = jnp.pad(meta, ((0, 0), (0, 0), (0, 4 - CAP), (0, 0)))
    meta = meta.reshape(groups, n_micro * 4, 2, LANES).swapaxes(1, 2)
    meta = meta.reshape(groups * 2 * n_micro * 4, LANES)
    row_flat = row_of.reshape(n_micro * n_pairs)
    above = lax.ppermute(row_flat, "section", [(i, i - 1) for i in range(1, n_section)])
    row_table = jnp.stack([above, row_flat], axis=1)

    n_rows = n_expert * CAP
    vmem = pl.BlockSpec(memory_space=pltpu.VMEM)
    smem = pl.BlockSpec(memory_space=pltpu.SMEM)
    hbm = pl.BlockSpec(memory_space=pl.ANY)
    dma = pltpu.SemaphoreType.DMA
    grads, sketch = pl.pallas_call(
        functools.partial(kernel, n_section, n_expert, groups),
        out_shape=(
            jax.ShapeDtypeStruct((n_micro, tok_dev, dk, LANES), BF16),
            jax.ShapeDtypeStruct((q_dev, r_dim // 2, 2 * r_dim), F32),
        ),
        in_specs=[smem, smem, vmem, vmem, vmem, vmem, hbm, hbm, hbm, hbm],
        out_specs=(vmem, vmem),
        scratch_shapes=[
            pltpu.VMEM((2 * hid, feat), BF16),
            pltpu.VMEM((hid + r_dim, feat), BF16),
            pltpu.VMEM((n_micro, n_slots, dk, LANES), BF16),
            pltpu.VMEM((n_micro, n_rows, dk, LANES), BF16),
            pltpu.VMEM((n_micro, n_slots, dk, LANES), BF16),
            pltpu.VMEM((n_micro, n_rows, dk, LANES), BF16),
            pltpu.VMEM((n_micro, n_rows, dk, LANES), BF16),
            pltpu.VMEM((n_rows, dk, LANES), BF16),
            pltpu.VMEM((n_rows, dk, LANES), BF16),
            pltpu.VMEM((n_rows, dk, LANES), BF16),
            pltpu.VMEM((n_rows, dk, LANES), BF16),
            pltpu.VMEM((n_expert * 16, LANES), F32),
            pltpu.VMEM((n_micro, tok_dev, dk, LANES), BF16),
            pltpu.VMEM((n_micro, tok_dev, dk, LANES), BF16),
            pltpu.VMEM((n_micro, tok_dev, dk, LANES), BF16),
            pltpu.VMEM((n_rows * dk, LANES), F32),
            pltpu.VMEM((n_rows, feat), BF16),
            pltpu.VMEM((n_rows, 2 * hid), BF16),
            pltpu.VMEM((n_micro, n_rows, hid), F32),
            pltpu.VMEM((n_micro, n_rows, hid), F32),
            pltpu.VMEM((n_micro, n_rows, r_dim), F32),
            pltpu.VMEM((n_micro, EXM, r_dim // 2, 2 * r_dim), F32),
            pltpu.VMEM((q_dev, hsplit, r_dim // 2, 2 * r_dim), F32),
            dma((4,)),
            dma((n_micro,)),
            dma((n_micro,)),
            dma((n_micro,)),
            dma((n_micro,)),
            dma((n_micro,)),
            dma((n_micro,)),
            dma((n_micro,)),
            dma(()),
            dma(()),
            dma((n_micro,)),
            dma((n_micro,)),
            dma((n_micro,)),
            dma((n_micro,)),
            dma((n_micro, EXM)),
            dma(()),
        ],
        compiler_params=pltpu.CompilerParams(collective_id=0, has_side_effects=True),
    )(
        tok_of_slot.reshape(n_micro * n_slots),
        row_table,
        saved_inputs.reshape(n_micro * tok_dev, dk, LANES),
        top_grad.reshape(n_micro, tok_dev, dk, LANES),
        meta,
        left_proj[0].T,
        gate_weight[0],
        up_weight[0],
        down_weight[0],
        right_proj[0].T,
    )
    return (
        grads.reshape(1, n_micro, tok_dev, feat),
        sketch.reshape(1, q_dev, r_dim * r_dim),
    )


def solution(mesh):
    placed = (
        P("section", None, "expert", None),
        P(None, "expert", None),
        P("section", None, "expert", None),
        P("section", None, "expert", None),
        P(None, "expert"),
        P("section", "expert", None),
        P("section", "expert", None),
        P("section", "expert", None),
        P("section", "expert", None),
        P("section", None, None),
    )
    return jax.shard_map(
        on_device,
        mesh=mesh,
        in_specs=placed,
        out_specs=(P("section", None, "expert", None), P("section", "expert", None)),
        check_vma=False,
    )
```

```python
import functools

import jax
import jax.numpy as jnp
from jax import lax
from jax.experimental import pallas as pl
from jax.experimental.pallas import tpu as pltpu
from jax.sharding import PartitionSpec as P

EXPERTS = 8
EXM = 4
CAP = 3
RING = 8
LANES = 128
F32 = jnp.float32
BF16 = jnp.bfloat16
MESH = pl.DeviceIdType.MESH


def far_first(n, me, n_expert):
    ring = RING if n_expert % RING == 0 else n_expert
    across = n_expert // ring

    def offset(rank, size):
        return size // 2 + (1 - 2 * lax.rem(rank, 2)) * ((rank + 1) // 2)

    z = lax.rem(lax.rem(me, ring) + offset(n // across, ring), ring)
    x = lax.rem(me // ring + offset(lax.rem(n, across), across), across)
    return x * ring + z


def kernel(
    n_section,
    n_expert,
    groups,
    tok_ref,
    row_ref,
    x_ref,
    top_ref,
    meta_ref,
    left_ref,
    gate_hbm,
    up_hbm,
    down_hbm,
    right_hbm,
    grads_ref,
    sketch_ref,
    wgu,
    wdr,
    xsend,
    xrecv,
    gsend,
    grecv,
    osend,
    crecv_a,
    crecv_b,
    frecv_a,
    frecv_b,
    metar,
    outgrad,
    resid,
    back,
    wide,
    rows,
    gcat,
    coef_g,
    coef_u,
    left_keep,
    psend,
    srecv,
    w_sem,
    xs_sem,
    xr_sem,
    gs_sem,
    gr_sem,
    os_sem,
    cr_sem,
    fr_sem,
    ms_sem,
    mr_sem,
    rs_sem,
    rr_sem,
    bs_sem,
    br_sem,
    ss_sem,
    sr_sem,
):
    crecv, frecv = (crecv_a, crecv_b), (frecv_a, frecv_b)
    sec = lax.axis_index("section")
    me = lax.axis_index("expert")
    hsplit = n_expert // groups
    n_micro, tok_dev = top_ref.shape[:2]
    n_slots = groups * CAP
    dk = x_ref.shape[1]
    hid = down_hbm.shape[0]
    top_k = row_ref.shape[0] // (n_micro * tok_dev)
    q_dev = n_micro * EXM * groups // n_expert
    r_dim = left_ref.shape[0]
    half = r_dim // 2
    last = sec == n_section - 1
    first = sec == 0

    loads = [
        pltpu.make_async_copy(gate_hbm, wgu.at[pl.ds(0, hid)], w_sem.at[0]),
        pltpu.make_async_copy(up_hbm, wgu.at[pl.ds(hid, hid)], w_sem.at[1]),
        pltpu.make_async_copy(down_hbm, wdr.at[pl.ds(0, hid)], w_sem.at[2]),
        pltpu.make_async_copy(right_hbm, wdr.at[pl.ds(hid, r_dim)], w_sem.at[3]),
    ]
    for load in loads:
        load.start()

    barrier = pltpu.get_barrier_semaphore()

    def greet(other, skip_me):
        def one(n, carry):
            to = far_first(n, me, n_expert)
            pl.semaphore_signal(
                barrier, inc=1, device_id={"section": other, "expert": to}, device_id_type=MESH
            )
            return carry

        lax.fori_loop(0, n_expert - 1 if skip_me else n_expert, one, 0)

    greet(sec, True)

    @pl.when(jnp.logical_not(first))
    def _():
        greet(sec - 1, False)

    @pl.when(jnp.logical_not(last))
    def _():
        greet(sec + 1, False)

    def xbuild(m, carry):
        for s in range(n_slots):
            xsend[m, s] = x_ref[m * tok_dev + tok_ref[m * n_slots + s]]
        return carry

    lax.fori_loop(0, n_micro, xbuild, 0)

    met = (
        n_expert - 1
        + jnp.where(first, 0, n_expert)
        + jnp.where(last, 0, n_expert)
    )
    pl.semaphore_wait(barrier, met)

    def spread(src, per, dst, send_sem, recv_sem):
        def one(n, carry):
            to = far_first(n, me, n_expert)
            pltpu.make_async_remote_copy(
                src_ref=src.at[pl.ds((to // hsplit) * per, per)],
                dst_ref=dst.at[pl.ds(me * per, per)],
                send_sem=send_sem,
                recv_sem=recv_sem,
                device_id={"section": sec, "expert": to},
                device_id_type=MESH,
            ).start()
            return carry

        lax.fori_loop(0, n_expert - 1, one, 0)
        pltpu.make_async_copy(
            src.at[pl.ds((me // hsplit) * per, per)], dst.at[pl.ds(me * per, per)], recv_sem
        ).start()

    def await_all(ref, sem):
        pltpu.make_async_copy(ref, ref, sem).wait()

    def dispatch(m):
        for s in range(n_slots):
            gsend[m, s] = outgrad[m, tok_ref[m * n_slots + s]]
        spread(gsend.at[m], CAP, grecv.at[m], gs_sem.at[m], gr_sem.at[m])

        @pl.when(jnp.logical_not(first))
        def _():
            pltpu.make_async_remote_copy(
                src_ref=outgrad.at[m],
                dst_ref=resid.at[m],
                send_sem=rs_sem.at[m],
                recv_sem=rr_sem.at[m],
                device_id={"section": sec - 1, "expert": me},
                device_id_type=MESH,
            ).start()

        @pl.when(jnp.logical_not(last))
        def _():
            pltpu.make_async_remote_copy(
                src_ref=outgrad.at[m],
                dst_ref=back.at[m],
                send_sem=bs_sem.at[m],
                recv_sem=br_sem.at[m],
                device_id={"section": sec + 1, "expert": me},
                device_id_type=MESH,
            ).start()

    def combined(m, t, base, parts, which):
        total = base
        for k in range(top_k):
            at = row_ref[m * tok_dev * top_k + t * top_k + k, which]
            for j in range(hsplit):
                total = total + parts[at + j * CAP].astype(F32)
        return total

    def start_micro(m, carry):
        spread(xsend.at[m], CAP, xrecv.at[m], xs_sem.at[m], xr_sem.at[m])

        @pl.when(m == 0)
        def _():
            spread(meta_ref, 16, metar, ms_sem, mr_sem)

        @pl.when(last)
        def _():
            outgrad[m] = top_ref[m]
            dispatch(m)

        return carry

    lax.fori_loop(0, n_micro, start_micro, 0)

    def by_row(ref, m):
        wide[...] = ref[m].reshape(n_expert * CAP * dk, LANES).astype(F32)
        for k in range(dk):
            for c in range(CAP):
                rows[pl.ds(c * n_expert, n_expert), pl.ds(k * LANES, LANES)] = wide[
                    pl.ds(c * dk + k, n_expert, stride=CAP * dk), :
                ].astype(BF16)

    def meta_of(m):
        return jnp.concatenate(
            [
                jnp.concatenate(
                    [metar[pl.ds(b * 8 + m * 4 + c, n_expert, stride=16), :] for b in range(2)],
                    axis=1,
                )
                for c in range(CAP)
            ],
            axis=0,
        )

    contract_last = (((1,), (1,)), ((), ()))
    for load in loads:
        load.wait()
    await_all(metar, mr_sem)

    def forward(m, carry):
        await_all(xrecv.at[m], xr_sem.at[m])
        by_row(xrecv, m)
        both = lax.dot_general(rows[...], wgu[...], contract_last, preferred_element_type=F32)
        pre_gate, pre_up = both[:, :hid], both[:, hid:]
        sigmoid_g = jax.nn.sigmoid(pre_gate)
        silu = pre_gate * sigmoid_g
        hidden = (silu * pre_up).astype(BF16)
        left_keep[m] = lax.dot_general(
            hidden, left_ref[...], contract_last, preferred_element_type=F32
        )
        weight = jnp.max(meta_of(m), axis=1, keepdims=True)
        coef_g[m] = weight * (pre_up * sigmoid_g * (1.0 + pre_gate * (1.0 - sigmoid_g)))
        coef_u[m] = weight * silu
        return carry

    @pl.when(jnp.logical_not(last))
    def _():
        lax.fori_loop(0, n_micro, forward, 0)

    def to_homes(m, other, skip_me, dst, recv_sem):
        def one(n, carry):
            to = far_first(n, me, n_expert)
            pltpu.make_async_remote_copy(
                src_ref=osend.at[m, pl.ds(to * CAP, CAP)],
                dst_ref=dst.at[pl.ds(me * CAP, CAP)],
                send_sem=os_sem.at[m],
                recv_sem=recv_sem,
                device_id={"section": other, "expert": to},
                device_id_type=MESH,
            ).start()
            return carry

        lax.fori_loop(0, n_expert - 1 if skip_me else n_expert, one, 0)

    def sketch_copies(m):
        mine = me // hsplit
        copies = []
        for ex in range(EXM):
            q = (m * EXM + ex) * groups + mine
            to = q // q_dev
            src = psend.at[m, ex]
            dst = srecv.at[lax.rem(q, q_dev), lax.rem(me, hsplit)]
            far = pltpu.make_async_remote_copy(
                src_ref=src,
                dst_ref=dst,
                send_sem=ss_sem.at[m, ex],
                recv_sem=sr_sem,
                device_id={"section": sec, "expert": to},
                device_id_type=MESH,
            )
            near = pltpu.make_async_copy(src, dst, sr_sem)
            copies.append((to, far, near))
        return copies

    def home(m, carry):
        await_all(resid.at[m], rr_sem.at[m])
        for which in range(n_micro):

            @pl.when(m == which)
            def _():
                await_all(crecv[which], cr_sem.at[which])
                for t in range(tok_dev):
                    base = resid[which, t].astype(F32)
                    total = combined(which, t, base, crecv[which], 0)
                    outgrad[which, t] = total.astype(BF16)

        dispatch(m)
        return carry

    @pl.when(jnp.logical_not(last))
    def _():
        lax.fori_loop(0, n_micro, home, 0)

    def step(m, carry):
        @pl.when(last)
        def _():
            forward(m, 0)

        await_all(grecv.at[m], gr_sem.at[m])
        by_row(grecv, m)
        both = lax.dot_general(
            rows[...], wdr[...], contract_last, preferred_element_type=F32
        )
        grad_hidden, right = both[:, :hid], both[:, hid:]
        gcat[:, pl.ds(0, hid)] = (grad_hidden * coef_g[m]).astype(BF16)
        gcat[:, pl.ds(hid, hid)] = (grad_hidden * coef_u[m]).astype(BF16)
        for n in range(dk // 2):
            part = jnp.dot(
                gcat[...], wgu[:, pl.ds(n * 2 * LANES, 2 * LANES)], preferred_element_type=F32
            )
            for b in range(2):
                k = n * 2 + b
                for c in range(CAP):
                    wide[pl.ds(c * dk + k, n_expert, stride=CAP * dk), :] = part[
                        c * n_expert : (c + 1) * n_expert, b * LANES : (b + 1) * LANES
                    ]
        osend[m] = wide[...].astype(BF16).reshape(n_expert * CAP, dk, LANES)

        for which in range(n_micro):

            @pl.when((m == which) & first)
            def _():
                to_homes(which, sec, True, frecv[which], fr_sem.at[which])
                pltpu.make_async_copy(
                    osend.at[which, pl.ds(me * CAP, CAP)],
                    frecv[which].at[pl.ds(me * CAP, CAP)],
                    fr_sem.at[which],
                ).start()

            @pl.when((m == which) & jnp.logical_not(first))
            def _():
                to_homes(which, sec - 1, False, crecv[which], cr_sem.at[which])

        right = jnp.concatenate([right] * EXM, axis=1) * meta_of(m)
        left = left_keep[m].astype(BF16)
        at_r = lax.broadcasted_iota(jnp.int32, (r_dim, r_dim), 0)
        at_c = lax.broadcasted_iota(jnp.int32, (r_dim, r_dim), 1)
        place = lax.rem(at_r, 2) * half + lax.div(at_r, 2)
        shuffle = jnp.where(at_c == place, 1.0, 0.0).astype(BF16)
        left = jnp.dot(left, shuffle, preferred_element_type=F32).astype(BF16)
        outer = lax.dot_general(
            left, right.astype(BF16), (((0,), (0,)), ((), ())), preferred_element_type=F32
        )
        for ex in range(EXM):
            block = outer[:, ex * r_dim : (ex + 1) * r_dim]
            psend[m, ex] = jnp.concatenate([block[:half], block[half:]], axis=1)
        for to, far, near in sketch_copies(m):

            @pl.when(to != me)
            def _():
                far.start()

            @pl.when(to == me)
            def _():
                near.start()

        return carry

    lax.fori_loop(0, n_micro, step, 0)

    @pl.when(first)
    def _():
        for m in range(n_micro):
            await_all(frecv[m], fr_sem.at[m])
            for t in range(tok_dev):
                total = combined(m, t, outgrad[m, t].astype(F32), frecv[m], 1)
                grads_ref[m, t] = total.astype(BF16)

    @pl.when(jnp.logical_not(first))
    def _():
        for m in range(n_micro):
            await_all(back.at[m], br_sem.at[m])
        grads_ref[...] = back[...]

    await_all(srecv, sr_sem)
    for q in range(q_dev):
        total = srecv[q, 0]
        for j in range(1, hsplit):
            total = total + srecv[q, j]
        sketch_ref[q] = total

    others = (n_expert - 1) * CAP
    await_all(metar.at[pl.ds(0, (n_expert - 1) * 16)], ms_sem)
    for m in range(n_micro):
        await_all(xrecv.at[m, pl.ds(0, others)], xs_sem.at[m])
        await_all(grecv.at[m, pl.ds(0, others)], gs_sem.at[m])

        @pl.when(first)
        def _():
            await_all(osend.at[m, pl.ds(0, others)], os_sem.at[m])

        @pl.when(jnp.logical_not(first))
        def _():
            await_all(osend.at[m], os_sem.at[m])
            await_all(outgrad.at[m], rs_sem.at[m])

        @pl.when(jnp.logical_not(last))
        def _():
            await_all(outgrad.at[m], bs_sem.at[m])

        for to, far, near in sketch_copies(m):

            @pl.when(to != me)
            def _():
                far.wait_send()


def on_device(
    saved_inputs,
    top_grad,
    expert_ids,
    route_weights,
    example_ids,
    gate_weight,
    up_weight,
    down_weight,
    left_proj,
    right_proj,
):
    n_section = lax.axis_size("section")
    n_expert = lax.axis_size("expert")
    groups = EXPERTS
    hsplit = n_expert // groups
    n_micro, tok_dev, feat = saved_inputs.shape[1:]
    top_k = expert_ids.shape[3]
    n_pairs = tok_dev * top_k
    n_slots = groups * CAP
    dk = feat // LANES
    hid = gate_weight.shape[1]
    r_dim = left_proj.shape[2]
    q_dev = n_micro * EXM * groups // n_expert

    ids = expert_ids[0].reshape(n_micro, n_pairs)
    weights = route_weights[0].reshape(n_micro, n_pairs).astype(F32)
    pair = jnp.arange(n_pairs, dtype=jnp.int32)
    same = (ids[:, :, None] == ids[:, None, :]) & (pair[:, None] > pair[None, :])[None]
    position = jnp.sum(same.astype(jnp.int32), axis=2)
    slot_of = ids * CAP + position
    row_of = ids * (hsplit * CAP) + position
    slots = jnp.arange(n_slots, dtype=jnp.int32)
    select = slot_of[:, None, :] == slots[None, :, None]
    tok_of_slot = jnp.sum(jnp.where(select, (pair // top_k)[None, None], 0), axis=2)
    slot_weight = jnp.sum(jnp.where(select, weights[:, None, :], 0.0), axis=2)
    example_pairs = jnp.repeat(example_ids, top_k, axis=1)
    slot_example = jnp.sum(jnp.where(select, example_pairs[:, None, :], 0), axis=2)
    lane_example = jnp.arange(EXM * r_dim, dtype=jnp.int32) // r_dim
    meta = jnp.where(
        slot_example[:, :, None] == lane_example[None, None], slot_weight[:, :, None], 0.0
    )
    meta = meta.reshape(n_micro, groups, CAP, EXM * r_dim).swapaxes(0, 1)
    meta = jnp.pad(meta, ((0, 0), (0, 0), (0, 4 - CAP), (0, 0)))
    meta = meta.reshape(groups, n_micro * 4, 2, LANES).swapaxes(1, 2)
    meta = meta.reshape(groups * 2 * n_micro * 4, LANES)
    row_flat = row_of.reshape(n_micro * n_pairs)
    above = lax.ppermute(row_flat, "section", [(i, i - 1) for i in range(1, n_section)])
    row_table = jnp.stack([above, row_flat], axis=1)

    n_rows = n_expert * CAP
    vmem = pl.BlockSpec(memory_space=pltpu.VMEM)
    smem = pl.BlockSpec(memory_space=pltpu.SMEM)
    hbm = pl.BlockSpec(memory_space=pl.ANY)
    dma = pltpu.SemaphoreType.DMA
    grads, sketch = pl.pallas_call(
        functools.partial(kernel, n_section, n_expert, groups),
        out_shape=(
            jax.ShapeDtypeStruct((n_micro, tok_dev, dk, LANES), BF16),
            jax.ShapeDtypeStruct((q_dev, r_dim // 2, 2 * r_dim), F32),
        ),
        in_specs=[smem, smem, vmem, vmem, vmem, vmem, hbm, hbm, hbm, hbm],
        out_specs=(vmem, vmem),
        scratch_shapes=[
            pltpu.VMEM((2 * hid, feat), BF16),
            pltpu.VMEM((hid + r_dim, feat), BF16),
            pltpu.VMEM((n_micro, n_slots, dk, LANES), BF16),
            pltpu.VMEM((n_micro, n_rows, dk, LANES), BF16),
            pltpu.VMEM((n_micro, n_slots, dk, LANES), BF16),
            pltpu.VMEM((n_micro, n_rows, dk, LANES), BF16),
            pltpu.VMEM((n_micro, n_rows, dk, LANES), BF16),
            pltpu.VMEM((n_rows, dk, LANES), BF16),
            pltpu.VMEM((n_rows, dk, LANES), BF16),
            pltpu.VMEM((n_rows, dk, LANES), BF16),
            pltpu.VMEM((n_rows, dk, LANES), BF16),
            pltpu.VMEM((n_expert * 16, LANES), F32),
            pltpu.VMEM((n_micro, tok_dev, dk, LANES), BF16),
            pltpu.VMEM((n_micro, tok_dev, dk, LANES), BF16),
            pltpu.VMEM((n_micro, tok_dev, dk, LANES), BF16),
            pltpu.VMEM((n_rows * dk, LANES), F32),
            pltpu.VMEM((n_rows, feat), BF16),
            pltpu.VMEM((n_rows, 2 * hid), BF16),
            pltpu.VMEM((n_micro, n_rows, hid), F32),
            pltpu.VMEM((n_micro, n_rows, hid), F32),
            pltpu.VMEM((n_micro, n_rows, r_dim), F32),
            pltpu.VMEM((n_micro, EXM, r_dim // 2, 2 * r_dim), F32),
            pltpu.VMEM((q_dev, hsplit, r_dim // 2, 2 * r_dim), F32),
            dma((4,)),
            dma((n_micro,)),
            dma((n_micro,)),
            dma((n_micro,)),
            dma((n_micro,)),
            dma((n_micro,)),
            dma((n_micro,)),
            dma((n_micro,)),
            dma(()),
            dma(()),
            dma((n_micro,)),
            dma((n_micro,)),
            dma((n_micro,)),
            dma((n_micro,)),
            dma((n_micro, EXM)),
            dma(()),
        ],
        compiler_params=pltpu.CompilerParams(collective_id=0, has_side_effects=True),
    )(
        tok_of_slot.reshape(n_micro * n_slots),
        row_table,
        saved_inputs.reshape(n_micro * tok_dev, dk, LANES),
        top_grad.reshape(n_micro, tok_dev, dk, LANES),
        meta,
        left_proj[0].T,
        gate_weight[0],
        up_weight[0],
        down_weight[0],
        right_proj[0].T,
    )
    return (
        grads.reshape(1, n_micro, tok_dev, feat),
        sketch.reshape(1, q_dev, r_dim * r_dim),
    )


def solution(mesh):
    placed = (
        P("section", None, "expert", None),
        P(None, "expert", None),
        P("section", None, "expert", None),
        P("section", None, "expert", None),
        P(None, "expert"),
        P("section", "expert", None),
        P("section", "expert", None),
        P("section", "expert", None),
        P("section", "expert", None),
        P("section", None, None),
    )
    return jax.shard_map(
        on_device,
        mesh=mesh,
        in_specs=placed,
        out_specs=(P("section", None, "expert", None), P("section", "expert", None)),
        check_vma=False,
    )
```

```python
import functools

import jax
import jax.numpy as jnp
from jax import lax
from jax.experimental import pallas as pl
from jax.experimental.pallas import tpu as pltpu
from jax.sharding import PartitionSpec as P

EXPERTS = 8
EXM = 4
CAP = 3
RING = 8
LANES = 128
F32 = jnp.float32
BF16 = jnp.bfloat16
MESH = pl.DeviceIdType.MESH


def far_first(n, me, n_expert):
    ring = RING if n_expert % RING == 0 else n_expert
    across = n_expert // ring

    def offset(rank, size):
        return size // 2 + (1 - 2 * lax.rem(rank, 2)) * ((rank + 1) // 2)

    z = lax.rem(lax.rem(me, ring) + offset(n // across, ring), ring)
    x = lax.rem(me // ring + offset(lax.rem(n, across), across), across)
    return x * ring + z


def kernel(
    n_section,
    n_expert,
    groups,
    tok_ref,
    row_ref,
    x_ref,
    top_ref,
    meta_ref,
    left_ref,
    gate_hbm,
    up_hbm,
    down_hbm,
    right_hbm,
    grads_ref,
    sketch_ref,
    wgu,
    wdr,
    xrows,
    xsend,
    xrecv,
    gsend,
    grecv,
    osend,
    crecv_a,
    crecv_b,
    frecv_a,
    frecv_b,
    metar,
    metaw,
    outgrad,
    resid,
    back,
    wide,
    rows,
    gcat,
    coef_g,
    coef_u,
    left_keep,
    right_keep,
    psend,
    srecv,
    w_sem,
    xs_sem,
    xr_sem,
    gs_sem,
    gr_sem,
    os_sem,
    cr_sem,
    fr_sem,
    ms_sem,
    mr_sem,
    rs_sem,
    rr_sem,
    bs_sem,
    br_sem,
    ss_sem,
    sr_sem,
):
    crecv, frecv = (crecv_a, crecv_b), (frecv_a, frecv_b)
    sec = lax.axis_index("section")
    me = lax.axis_index("expert")
    hsplit = n_expert // groups
    n_micro, tok_dev, dk, _ = outgrad.shape
    n_slots = groups * CAP
    hid = down_hbm.shape[0]
    top_k = row_ref.shape[0] // (2 * n_micro * tok_dev)
    q_dev = n_micro * EXM * groups // n_expert
    r_dim = left_ref.shape[0]
    half = r_dim // 2
    last = sec == n_section - 1
    first = sec == 0

    loads = [
        pltpu.make_async_copy(gate_hbm, wgu.at[pl.ds(0, hid)], w_sem.at[0]),
        pltpu.make_async_copy(up_hbm, wgu.at[pl.ds(hid, hid)], w_sem.at[1]),
        pltpu.make_async_copy(down_hbm, wdr.at[pl.ds(0, hid)], w_sem.at[2]),
        pltpu.make_async_copy(right_hbm, wdr.at[pl.ds(hid, r_dim)], w_sem.at[3]),
    ]
    for load in loads:
        load.start()

    barrier = pltpu.get_barrier_semaphore()

    def greet(other, skip_me):
        def one(n, carry):
            to = far_first(n, me, n_expert)
            pl.semaphore_signal(
                barrier, inc=1, device_id={"section": other, "expert": to}, device_id_type=MESH
            )
            return carry

        lax.fori_loop(0, n_expert - 1 if skip_me else n_expert, one, 0)

    greet(sec, True)

    @pl.when(jnp.logical_not(first))
    def _():
        greet(sec - 1, False)

    @pl.when(jnp.logical_not(last))
    def _():
        greet(sec + 1, False)

    def tiles_of(ref):
        n = n_micro * tok_dev
        for k in range(dk):
            wide[pl.ds(k, n, stride=dk), :] = ref[:, pl.ds(k * LANES, LANES)].astype(F32)
        return wide[pl.ds(0, n * dk), :].astype(BF16).reshape(n, dk, LANES)

    xrows[...] = tiles_of(x_ref)

    @pl.when(last)
    def _():
        outgrad[...] = tiles_of(top_ref).reshape(n_micro, tok_dev, dk, LANES)

    def xbuild(m, carry):
        for s in range(n_slots):
            xsend[m, s] = xrows[m * tok_dev + tok_ref[m * n_slots + s]]
        return carry

    lax.fori_loop(0, n_micro, xbuild, 0)

    met = (
        n_expert - 1
        + jnp.where(first, 0, n_expert)
        + jnp.where(last, 0, n_expert)
    )
    pl.semaphore_wait(barrier, met)

    def spread(src, per, dst, send_sem, recv_sem):
        def one(n, carry):
            to = far_first(n, me, n_expert)
            pltpu.make_async_remote_copy(
                src_ref=src.at[pl.ds((to // hsplit) * per, per)],
                dst_ref=dst.at[pl.ds(me * per, per)],
                send_sem=send_sem,
                recv_sem=recv_sem,
                device_id={"section": sec, "expert": to},
                device_id_type=MESH,
            ).start()
            return carry

        for n in range(n_expert - 1):
            one(n, 0)
        pltpu.make_async_copy(
            src.at[pl.ds((me // hsplit) * per, per)], dst.at[pl.ds(me * per, per)], recv_sem
        ).start()

    def await_all(ref, sem):
        pltpu.make_async_copy(ref, ref, sem).wait()

    def dispatch(m):
        for s in range(n_slots):
            gsend[m, s] = outgrad[m, tok_ref[m * n_slots + s]]
        spread(gsend.at[m], CAP, grecv.at[m], gs_sem.at[m], gr_sem.at[m])

        @pl.when(jnp.logical_not(first))
        def _():
            pltpu.make_async_remote_copy(
                src_ref=outgrad.at[m],
                dst_ref=resid.at[m],
                send_sem=rs_sem.at[m],
                recv_sem=rr_sem.at[m],
                device_id={"section": sec - 1, "expert": me},
                device_id_type=MESH,
            ).start()

        @pl.when(jnp.logical_not(last))
        def _():
            pltpu.make_async_remote_copy(
                src_ref=outgrad.at[m],
                dst_ref=back.at[m],
                send_sem=bs_sem.at[m],
                recv_sem=br_sem.at[m],
                device_id={"section": sec + 1, "expert": me},
                device_id_type=MESH,
            ).start()

    def combined(m, t, base, parts, which):
        total = base
        for k in range(top_k):
            at = row_ref[((which * n_micro + m) * top_k + k) * tok_dev + t]
            for j in range(hsplit):
                total = total + parts[at + j * CAP].astype(F32)
        return total

    def send_inputs(m):
        spread(xsend.at[m], CAP, xrecv.at[m], xs_sem.at[m], xr_sem.at[m])

    send_inputs(0)
    spread(meta_ref, 16, metar, ms_sem, mr_sem)

    @pl.when(last)
    def _():
        def start_micro(m, carry):
            @pl.when(m > 0)
            def _():
                send_inputs(m)

            dispatch(m)
            return carry

        lax.fori_loop(0, n_micro, start_micro, 0)

    def by_row(ref, m):
        wide[...] = ref[m].reshape(n_expert * CAP * dk, LANES).astype(F32)
        for k in range(dk):
            for c in range(CAP):
                rows[pl.ds(c * n_expert, n_expert), pl.ds(k * LANES, LANES)] = wide[
                    pl.ds(c * dk + k, n_expert, stride=CAP * dk), :
                ].astype(BF16)

    def meta_of(m):
        return jnp.concatenate(
            [
                jnp.concatenate(
                    [metaw[pl.ds(b * 8 + m * 4 + c, n_expert, stride=16), :] for b in range(2)],
                    axis=1,
                )
                for c in range(CAP)
            ],
            axis=0,
        )

    contract_last = (((1,), (1,)), ((), ()))
    for load in loads:
        load.wait()
    await_all(metar, mr_sem)
    metaw[...] = metar[...].astype(F32)

    def forward(m, carry):
        await_all(xrecv.at[m], xr_sem.at[m])
        by_row(xrecv, m)
        both = lax.dot_general(rows[...], wgu[...], contract_last, preferred_element_type=F32)
        pre_gate, pre_up = both[:, :hid], both[:, hid:]
        sigmoid_g = jax.nn.sigmoid(pre_gate)
        silu = pre_gate * sigmoid_g
        hidden = (silu * pre_up).astype(BF16)
        left_keep[m] = lax.dot_general(
            hidden, left_ref[...], contract_last, preferred_element_type=F32
        )
        weight = jnp.max(meta_of(m), axis=1, keepdims=True)
        coef_g[m] = weight * (pre_up * sigmoid_g * (1.0 + pre_gate * (1.0 - sigmoid_g)))
        coef_u[m] = weight * silu
        return carry

    @pl.when(jnp.logical_not(last))
    def _():
        def prepare(m, carry):
            forward(m, 0)

            @pl.when(m + 1 < n_micro)
            def _():
                send_inputs(m + 1)

            return carry

        lax.fori_loop(0, n_micro, prepare, 0)

    def to_homes(m, other, skip_me, dst, recv_sem):
        def one(n, carry):
            to = far_first(n, me, n_expert)
            pltpu.make_async_remote_copy(
                src_ref=osend.at[m, pl.ds(to * CAP, CAP)],
                dst_ref=dst.at[pl.ds(me * CAP, CAP)],
                send_sem=os_sem.at[m],
                recv_sem=recv_sem,
                device_id={"section": other, "expert": to},
                device_id_type=MESH,
            ).start()
            return carry

        for n in range(n_expert - 1 if skip_me else n_expert):
            one(n, 0)

    def sketch_copies(m):
        mine = me // hsplit
        copies = []
        for ex in range(EXM):
            q = (m * EXM + ex) * groups + mine
            to = q // q_dev
            src = psend.at[m, ex]
            dst = srecv.at[lax.rem(q, q_dev), lax.rem(me, hsplit)]
            far = pltpu.make_async_remote_copy(
                src_ref=src,
                dst_ref=dst,
                send_sem=ss_sem.at[m, ex],
                recv_sem=sr_sem,
                device_id={"section": sec, "expert": to},
                device_id_type=MESH,
            )
            near = pltpu.make_async_copy(src, dst, sr_sem)
            copies.append((to, far, near))
        return copies

    def home(m, carry):
        await_all(resid.at[m], rr_sem.at[m])
        for which in range(n_micro):

            @pl.when(m == which)
            def _():
                await_all(crecv[which], cr_sem.at[which])
                for t in range(tok_dev):
                    base = resid[which, t].astype(F32)
                    total = combined(which, t, base, crecv[which], 0)
                    outgrad[which, t] = total.astype(BF16)

        dispatch(m)
        return carry

    @pl.when(jnp.logical_not(last))
    def _():
        lax.fori_loop(0, n_micro, home, 0)

    def step(m, carry):
        @pl.when(last)
        def _():
            forward(m, 0)

        await_all(grecv.at[m], gr_sem.at[m])
        by_row(grecv, m)
        both = lax.dot_general(
            rows[...], wdr[...], contract_last, preferred_element_type=F32
        )
        grad_hidden, right = both[:, :hid], both[:, hid:]
        gcat[:, pl.ds(0, hid)] = (grad_hidden * coef_g[m]).astype(BF16)
        gcat[:, pl.ds(hid, hid)] = (grad_hidden * coef_u[m]).astype(BF16)
        for n in range(dk // 2):
            part = jnp.dot(
                gcat[...], wgu[:, pl.ds(n * 2 * LANES, 2 * LANES)], preferred_element_type=F32
            )
            for b in range(2):
                k = n * 2 + b
                for c in range(CAP):
                    wide[pl.ds(c * dk + k, n_expert, stride=CAP * dk), :] = part[
                        c * n_expert : (c + 1) * n_expert, b * LANES : (b + 1) * LANES
                    ]
        osend[m] = wide[...].astype(BF16).reshape(n_expert * CAP, dk, LANES)

        for which in range(n_micro):

            @pl.when((m == which) & first)
            def _():
                to_homes(which, sec, True, frecv[which], fr_sem.at[which])
                pltpu.make_async_copy(
                    osend.at[which, pl.ds(me * CAP, CAP)],
                    frecv[which].at[pl.ds(me * CAP, CAP)],
                    fr_sem.at[which],
                ).start()

            @pl.when((m == which) & jnp.logical_not(first))
            def _():
                to_homes(which, sec - 1, False, crecv[which], cr_sem.at[which])

        right_keep[m] = right
        return carry

    def outer_of(m, carry):
        right = jnp.concatenate([right_keep[m]] * EXM, axis=1) * meta_of(m)
        left = left_keep[m].astype(BF16)
        at_r = lax.broadcasted_iota(jnp.int32, (r_dim, r_dim), 0)
        at_c = lax.broadcasted_iota(jnp.int32, (r_dim, r_dim), 1)
        place = lax.rem(at_r, 2) * half + lax.div(at_r, 2)
        shuffle = jnp.where(at_c == place, 1.0, 0.0).astype(BF16)
        left = jnp.dot(left, shuffle, preferred_element_type=F32).astype(BF16)
        outer = lax.dot_general(
            left, right.astype(BF16), (((0,), (0,)), ((), ())), preferred_element_type=F32
        )
        for ex in range(EXM):
            block = outer[:, ex * r_dim : (ex + 1) * r_dim]
            psend[m, ex] = jnp.concatenate([block[:half], block[half:]], axis=1)
        for to, far, near in sketch_copies(m):

            @pl.when(to != me)
            def _():
                far.start()

            @pl.when(to == me)
            def _():
                near.start()

        return carry

    lax.fori_loop(0, n_micro, step, 0)
    lax.fori_loop(0, n_micro, outer_of, 0)

    @pl.when(first)
    def _():
        for m in range(n_micro):
            await_all(frecv[m], fr_sem.at[m])
            for t in range(tok_dev):
                total = combined(m, t, outgrad[m, t].astype(F32), frecv[m], 1)
                grads_ref[m, t] = total.astype(BF16)

    @pl.when(jnp.logical_not(first))
    def _():
        for m in range(n_micro):
            await_all(back.at[m], br_sem.at[m])
        grads_ref[...] = back[...]

    await_all(srecv, sr_sem)
    for q in range(q_dev):
        total = srecv[q, 0]
        for j in range(1, hsplit):
            total = total + srecv[q, j]
        sketch_ref[q] = total

    others = (n_expert - 1) * CAP
    await_all(metar.at[pl.ds(0, (n_expert - 1) * 16)], ms_sem)
    for m in range(n_micro):
        await_all(xrecv.at[m, pl.ds(0, others)], xs_sem.at[m])
        await_all(grecv.at[m, pl.ds(0, others)], gs_sem.at[m])

        @pl.when(first)
        def _():
            await_all(osend.at[m, pl.ds(0, others)], os_sem.at[m])

        @pl.when(jnp.logical_not(first))
        def _():
            await_all(osend.at[m], os_sem.at[m])
            await_all(outgrad.at[m], rs_sem.at[m])

        @pl.when(jnp.logical_not(last))
        def _():
            await_all(outgrad.at[m], bs_sem.at[m])

        for to, far, near in sketch_copies(m):

            @pl.when(to != me)
            def _():
                far.wait_send()


def on_device(
    saved_inputs,
    top_grad,
    expert_ids,
    route_weights,
    example_ids,
    gate_weight,
    up_weight,
    down_weight,
    left_proj,
    right_proj,
):
    n_section = lax.axis_size("section")
    n_expert = lax.axis_size("expert")
    groups = EXPERTS
    hsplit = n_expert // groups
    n_micro, tok_dev, feat = saved_inputs.shape[1:]
    top_k = expert_ids.shape[3]
    n_pairs = tok_dev * top_k
    n_slots = groups * CAP
    dk = feat // LANES
    hid = gate_weight.shape[1]
    r_dim = left_proj.shape[2]
    q_dev = n_micro * EXM * groups // n_expert

    ids = expert_ids[0].swapaxes(1, 2).reshape(n_micro, n_pairs)
    weights = route_weights[0].swapaxes(1, 2).reshape(n_micro, n_pairs).astype(F32)
    pair = jnp.arange(n_pairs, dtype=jnp.int32)
    same = (ids[:, :, None] == ids[:, None, :]) & (pair[:, None] > pair[None, :])[None]
    position = jnp.sum(same.astype(jnp.int32), axis=2)
    slot_of = ids * CAP + position
    row_of = ids * (hsplit * CAP) + position
    slots = jnp.arange(n_slots, dtype=jnp.int32)
    select = slot_of[:, None, :] == slots[None, :, None]
    tok_of_slot = jnp.sum(jnp.where(select, (pair % tok_dev)[None, None], 0), axis=2)
    slot_weight = jnp.sum(jnp.where(select, weights[:, None, :], 0.0), axis=2)
    example_pairs = jnp.concatenate([example_ids] * top_k, axis=1)
    slot_example = jnp.sum(jnp.where(select, example_pairs[:, None, :], 0), axis=2)
    lane_example = jnp.arange(EXM * r_dim, dtype=jnp.int32) // r_dim
    meta = jnp.where(
        slot_example[:, :, None] == lane_example[None, None], slot_weight[:, :, None], 0.0
    )
    meta = meta.reshape(n_micro, groups, CAP, EXM * r_dim).swapaxes(0, 1)
    meta = jnp.pad(meta, ((0, 0), (0, 0), (0, 4 - CAP), (0, 0)))
    meta = meta.reshape(groups, n_micro * 4, 2, LANES).swapaxes(1, 2)
    meta = meta.reshape(groups * 2 * n_micro * 4, LANES).astype(BF16)
    row_flat = row_of.reshape(n_micro * n_pairs)
    above = lax.ppermute(row_flat, "section", [(i, i - 1) for i in range(1, n_section)])
    row_table = jnp.concatenate([above, row_flat])

    n_rows = n_expert * CAP
    vmem = pl.BlockSpec(memory_space=pltpu.VMEM)
    smem = pl.BlockSpec(memory_space=pltpu.SMEM)
    hbm = pl.BlockSpec(memory_space=pl.ANY)
    dma = pltpu.SemaphoreType.DMA
    grads, sketch = pl.pallas_call(
        functools.partial(kernel, n_section, n_expert, groups),
        out_shape=(
            jax.ShapeDtypeStruct((n_micro, tok_dev, dk, LANES), BF16),
            jax.ShapeDtypeStruct((q_dev, r_dim // 2, 2 * r_dim), F32),
        ),
        in_specs=[smem, smem, vmem, vmem, vmem, vmem, hbm, hbm, hbm, hbm],
        out_specs=(vmem, vmem),
        scratch_shapes=[
            pltpu.VMEM((2 * hid, feat), BF16),
            pltpu.VMEM((hid + r_dim, feat), BF16),
            pltpu.VMEM((n_micro * tok_dev, dk, LANES), BF16),
            pltpu.VMEM((n_micro, n_slots, dk, LANES), BF16),
            pltpu.VMEM((n_micro, n_rows, dk, LANES), BF16),
            pltpu.VMEM((n_micro, n_slots, dk, LANES), BF16),
            pltpu.VMEM((n_micro, n_rows, dk, LANES), BF16),
            pltpu.VMEM((n_micro, n_rows, dk, LANES), BF16),
            pltpu.VMEM((n_rows, dk, LANES), BF16),
            pltpu.VMEM((n_rows, dk, LANES), BF16),
            pltpu.VMEM((n_rows, dk, LANES), BF16),
            pltpu.VMEM((n_rows, dk, LANES), BF16),
            pltpu.VMEM((n_expert * 16, LANES), BF16),
            pltpu.VMEM((n_expert * 16, LANES), F32),
            pltpu.VMEM((n_micro, tok_dev, dk, LANES), BF16),
            pltpu.VMEM((n_micro, tok_dev, dk, LANES), BF16),
            pltpu.VMEM((n_micro, tok_dev, dk, LANES), BF16),
            pltpu.VMEM((n_rows * dk, LANES), F32),
            pltpu.VMEM((n_rows, feat), BF16),
            pltpu.VMEM((n_rows, 2 * hid), BF16),
            pltpu.VMEM((n_micro, n_rows, hid), F32),
            pltpu.VMEM((n_micro, n_rows, hid), F32),
            pltpu.VMEM((n_micro, n_rows, r_dim), F32),
            pltpu.VMEM((n_micro, n_rows, r_dim), F32),
            pltpu.VMEM((n_micro, EXM, r_dim // 2, 2 * r_dim), F32),
            pltpu.VMEM((q_dev, hsplit, r_dim // 2, 2 * r_dim), F32),
            dma((4,)),
            dma((n_micro,)),
            dma((n_micro,)),
            dma((n_micro,)),
            dma((n_micro,)),
            dma((n_micro,)),
            dma((n_micro,)),
            dma((n_micro,)),
            dma(()),
            dma(()),
            dma((n_micro,)),
            dma((n_micro,)),
            dma((n_micro,)),
            dma((n_micro,)),
            dma((n_micro, EXM)),
            dma(()),
        ],
        compiler_params=pltpu.CompilerParams(collective_id=0, has_side_effects=True),
    )(
        tok_of_slot.reshape(n_micro * n_slots),
        row_table,
        saved_inputs.reshape(n_micro * tok_dev, feat),
        top_grad.reshape(n_micro * tok_dev, feat),
        meta,
        left_proj[0].T,
        gate_weight[0],
        up_weight[0],
        down_weight[0],
        right_proj[0].T,
    )
    return (
        grads.reshape(1, n_micro, tok_dev, feat),
        sketch.reshape(1, q_dev, r_dim * r_dim),
    )


def solution(mesh):
    placed = (
        P("section", None, "expert", None),
        P(None, "expert", None),
        P("section", None, "expert", None),
        P("section", None, "expert", None),
        P(None, "expert"),
        P("section", "expert", None),
        P("section", "expert", None),
        P("section", "expert", None),
        P("section", "expert", None),
        P("section", None, None),
    )
    return jax.shard_map(
        on_device,
        mesh=mesh,
        in_specs=placed,
        out_specs=(P("section", None, "expert", None), P("section", "expert", None)),
        check_vma=False,
    )
```

```python
import functools

import jax
import jax.numpy as jnp
from jax import lax
from jax.experimental import pallas as pl
from jax.experimental.pallas import tpu as pltpu
from jax.sharding import PartitionSpec as P

EXPERTS = 8
EXM = 4
CAP = 3
RING = 8
LANES = 128
F32 = jnp.float32
BF16 = jnp.bfloat16
MESH = pl.DeviceIdType.MESH


def far_first(n, me, n_expert):
    ring = RING if n_expert % RING == 0 else n_expert
    across = n_expert // ring

    def offset(rank, size):
        return size // 2 + (1 - 2 * lax.rem(rank, 2)) * ((rank + 1) // 2)

    z = lax.rem(lax.rem(me, ring) + offset(lax.rem(n, ring), ring), ring)
    x = lax.rem(me // ring + offset(n // ring, across), across)
    return x * ring + z


def kernel(
    n_section,
    n_expert,
    groups,
    tok_ref,
    row_ref,
    x_ref,
    top_ref,
    meta_ref,
    left_ref,
    gate_hbm,
    up_hbm,
    down_hbm,
    right_hbm,
    grads_ref,
    sketch_ref,
    wgu,
    wdr,
    xrows,
    xsend,
    xrecv,
    gsend,
    grecv,
    osend,
    crecv_a,
    crecv_b,
    frecv_a,
    frecv_b,
    metar,
    metaw,
    outgrad,
    resid,
    back,
    wide,
    rows,
    gcat,
    coef_g,
    coef_u,
    left_keep,
    right_keep,
    psend,
    srecv,
    w_sem,
    xs_sem,
    xr_sem,
    gs_sem,
    gr_sem,
    os_sem,
    cr_sem,
    fr_sem,
    ms_sem,
    mr_sem,
    rs_sem,
    rr_sem,
    bs_sem,
    br_sem,
    ss_sem,
    sr_sem,
):
    crecv, frecv = (crecv_a, crecv_b), (frecv_a, frecv_b)
    sec = lax.axis_index("section")
    me = lax.axis_index("expert")
    hsplit = n_expert // groups
    n_micro, tok_dev, dk, _ = outgrad.shape
    n_slots = groups * CAP
    hid = down_hbm.shape[0]
    top_k = row_ref.shape[0] // (2 * n_micro * tok_dev)
    q_dev = n_micro * EXM * groups // n_expert
    r_dim = left_ref.shape[0]
    half = r_dim // 2
    last = sec == n_section - 1
    first = sec == 0

    loads = [
        pltpu.make_async_copy(gate_hbm, wgu.at[pl.ds(0, hid)], w_sem.at[0]),
        pltpu.make_async_copy(up_hbm, wgu.at[pl.ds(hid, hid)], w_sem.at[1]),
        pltpu.make_async_copy(down_hbm, wdr.at[pl.ds(0, hid)], w_sem.at[2]),
        pltpu.make_async_copy(right_hbm, wdr.at[pl.ds(hid, r_dim)], w_sem.at[3]),
    ]
    for load in loads:
        load.start()

    barrier = pltpu.get_barrier_semaphore()

    def greet(other, skip_me):
        def one(n, carry):
            to = far_first(n, me, n_expert)
            pl.semaphore_signal(
                barrier, inc=1, device_id={"section": other, "expert": to}, device_id_type=MESH
            )
            return carry

        lax.fori_loop(0, n_expert - 1 if skip_me else n_expert, one, 0)

    greet(sec, True)

    @pl.when(jnp.logical_not(first))
    def _():
        greet(sec - 1, False)

    @pl.when(jnp.logical_not(last))
    def _():
        greet(sec + 1, False)

    def tiles_of(ref):
        n = n_micro * tok_dev
        for k in range(dk):
            wide[pl.ds(k, n, stride=dk), :] = ref[:, pl.ds(k * LANES, LANES)].astype(F32)
        return wide[pl.ds(0, n * dk), :].astype(BF16).reshape(n, dk, LANES)

    xrows[...] = tiles_of(x_ref)

    @pl.when(last)
    def _():
        outgrad[...] = tiles_of(top_ref).reshape(n_micro, tok_dev, dk, LANES)

    def xbuild(m, carry):
        for s in range(n_slots):
            xsend[m, s] = xrows[m * tok_dev + tok_ref[m * n_slots + s]]
        return carry

    lax.fori_loop(0, n_micro, xbuild, 0)

    met = (
        n_expert - 1
        + jnp.where(first, 0, n_expert)
        + jnp.where(last, 0, n_expert)
    )
    pl.semaphore_wait(barrier, met)

    def spread(src, per, dst, send_sem, recv_sem):
        def one(n, carry):
            to = far_first(n, me, n_expert)
            pltpu.make_async_remote_copy(
                src_ref=src.at[pl.ds((to // hsplit) * per, per)],
                dst_ref=dst.at[pl.ds(me * per, per)],
                send_sem=send_sem,
                recv_sem=recv_sem,
                device_id={"section": sec, "expert": to},
                device_id_type=MESH,
            ).start()
            return carry

        for n in range(n_expert - 1):
            one(n, 0)
        pltpu.make_async_copy(
            src.at[pl.ds((me // hsplit) * per, per)], dst.at[pl.ds(me * per, per)], recv_sem
        ).start()

    def await_all(ref, sem):
        pltpu.make_async_copy(ref, ref, sem).wait()

    def dispatch(m):
        for s in range(n_slots):
            gsend[m, s] = outgrad[m, tok_ref[m * n_slots + s]]
        spread(gsend.at[m], CAP, grecv.at[m], gs_sem.at[m], gr_sem.at[m])

        @pl.when(jnp.logical_not(first))
        def _():
            pltpu.make_async_remote_copy(
                src_ref=outgrad.at[m],
                dst_ref=resid.at[m],
                send_sem=rs_sem.at[m],
                recv_sem=rr_sem.at[m],
                device_id={"section": sec - 1, "expert": me},
                device_id_type=MESH,
            ).start()

        @pl.when(jnp.logical_not(last))
        def _():
            pltpu.make_async_remote_copy(
                src_ref=outgrad.at[m],
                dst_ref=back.at[m],
                send_sem=bs_sem.at[m],
                recv_sem=br_sem.at[m],
                device_id={"section": sec + 1, "expert": me},
                device_id_type=MESH,
            ).start()

    def combined(m, t, base, parts, which):
        total = base
        for k in range(top_k):
            at = row_ref[((which * n_micro + m) * top_k + k) * tok_dev + t]
            for j in range(hsplit):
                total = total + parts[at + j * CAP].astype(F32)
        return total

    def send_inputs(m):
        spread(xsend.at[m], CAP, xrecv.at[m], xs_sem.at[m], xr_sem.at[m])

    send_inputs(0)
    spread(meta_ref, 16, metar, ms_sem, mr_sem)

    @pl.when(last)
    def _():
        def start_micro(m, carry):
            @pl.when(m > 0)
            def _():
                send_inputs(m)

            dispatch(m)
            return carry

        lax.fori_loop(0, n_micro, start_micro, 0)

    def by_row(ref, m):
        wide[...] = ref[m].reshape(n_expert * CAP * dk, LANES).astype(F32)
        for k in range(dk):
            for c in range(CAP):
                rows[pl.ds(c * n_expert, n_expert), pl.ds(k * LANES, LANES)] = wide[
                    pl.ds(c * dk + k, n_expert, stride=CAP * dk), :
                ].astype(BF16)

    def meta_of(m):
        return jnp.concatenate(
            [
                jnp.concatenate(
                    [metaw[pl.ds(b * 8 + m * 4 + c, n_expert, stride=16), :] for b in range(2)],
                    axis=1,
                )
                for c in range(CAP)
            ],
            axis=0,
        )

    contract_last = (((1,), (1,)), ((), ()))
    for load in loads:
        load.wait()
    await_all(metar, mr_sem)
    metaw[...] = metar[...].astype(F32)

    def forward(m, carry):
        await_all(xrecv.at[m], xr_sem.at[m])
        by_row(xrecv, m)
        both = lax.dot_general(rows[...], wgu[...], contract_last, preferred_element_type=F32)
        pre_gate, pre_up = both[:, :hid], both[:, hid:]
        sigmoid_g = jax.nn.sigmoid(pre_gate)
        silu = pre_gate * sigmoid_g
        hidden = (silu * pre_up).astype(BF16)
        left_keep[m] = lax.dot_general(
            hidden, left_ref[...], contract_last, preferred_element_type=F32
        )
        weight = jnp.max(meta_of(m), axis=1, keepdims=True)
        coef_g[m] = weight * (pre_up * sigmoid_g * (1.0 + pre_gate * (1.0 - sigmoid_g)))
        coef_u[m] = weight * silu
        return carry

    @pl.when(jnp.logical_not(last))
    def _():
        def prepare(m, carry):
            forward(m, 0)

            @pl.when(m + 1 < n_micro)
            def _():
                send_inputs(m + 1)

            return carry

        lax.fori_loop(0, n_micro, prepare, 0)

    def to_homes(m, other, skip_me, dst, recv_sem):
        def one(n, carry):
            to = far_first(n, me, n_expert)
            pltpu.make_async_remote_copy(
                src_ref=osend.at[m, pl.ds(to * CAP, CAP)],
                dst_ref=dst.at[pl.ds(me * CAP, CAP)],
                send_sem=os_sem.at[m],
                recv_sem=recv_sem,
                device_id={"section": other, "expert": to},
                device_id_type=MESH,
            ).start()
            return carry

        for n in range(n_expert - 1 if skip_me else n_expert):
            one(n, 0)

    def sketch_copies(m):
        mine = me // hsplit
        copies = []
        for ex in range(EXM):
            q = (m * EXM + ex) * groups + mine
            to = q // q_dev
            src = psend.at[m, ex]
            dst = srecv.at[lax.rem(q, q_dev), lax.rem(me, hsplit)]
            far = pltpu.make_async_remote_copy(
                src_ref=src,
                dst_ref=dst,
                send_sem=ss_sem.at[m, ex],
                recv_sem=sr_sem,
                device_id={"section": sec, "expert": to},
                device_id_type=MESH,
            )
            near = pltpu.make_async_copy(src, dst, sr_sem)
            copies.append((to, far, near))
        return copies

    def home(m, carry):
        await_all(resid.at[m], rr_sem.at[m])
        for which in range(n_micro):

            @pl.when(m == which)
            def _():
                await_all(crecv[which], cr_sem.at[which])
                for t in range(tok_dev):
                    base = resid[which, t].astype(F32)
                    total = combined(which, t, base, crecv[which], 0)
                    outgrad[which, t] = total.astype(BF16)

        dispatch(m)
        return carry

    @pl.when(jnp.logical_not(last))
    def _():
        lax.fori_loop(0, n_micro, home, 0)

    def step(m, carry):
        @pl.when(last)
        def _():
            forward(m, 0)

        await_all(grecv.at[m], gr_sem.at[m])
        by_row(grecv, m)
        both = lax.dot_general(
            rows[...], wdr[...], contract_last, preferred_element_type=F32
        )
        grad_hidden, right = both[:, :hid], both[:, hid:]
        gcat[:, pl.ds(0, hid)] = (grad_hidden * coef_g[m]).astype(BF16)
        gcat[:, pl.ds(hid, hid)] = (grad_hidden * coef_u[m]).astype(BF16)
        for n in range(dk // 2):
            part = jnp.dot(
                gcat[...], wgu[:, pl.ds(n * 2 * LANES, 2 * LANES)], preferred_element_type=F32
            )
            for b in range(2):
                k = n * 2 + b
                for c in range(CAP):
                    wide[pl.ds(c * dk + k, n_expert, stride=CAP * dk), :] = part[
                        c * n_expert : (c + 1) * n_expert, b * LANES : (b + 1) * LANES
                    ]
        osend[m] = wide[...].astype(BF16).reshape(n_expert * CAP, dk, LANES)

        for which in range(n_micro):

            @pl.when((m == which) & first)
            def _():
                to_homes(which, sec, True, frecv[which], fr_sem.at[which])
                pltpu.make_async_copy(
                    osend.at[which, pl.ds(me * CAP, CAP)],
                    frecv[which].at[pl.ds(me * CAP, CAP)],
                    fr_sem.at[which],
                ).start()

            @pl.when((m == which) & jnp.logical_not(first))
            def _():
                to_homes(which, sec - 1, False, crecv[which], cr_sem.at[which])

        right_keep[m] = right
        return carry

    def outer_of(m, carry):
        right = jnp.concatenate([right_keep[m]] * EXM, axis=1) * meta_of(m)
        left = left_keep[m].astype(BF16)
        at_r = lax.broadcasted_iota(jnp.int32, (r_dim, r_dim), 0)
        at_c = lax.broadcasted_iota(jnp.int32, (r_dim, r_dim), 1)
        place = lax.rem(at_r, 2) * half + lax.div(at_r, 2)
        shuffle = jnp.where(at_c == place, 1.0, 0.0).astype(BF16)
        left = jnp.dot(left, shuffle, preferred_element_type=F32).astype(BF16)
        outer = lax.dot_general(
            left, right.astype(BF16), (((0,), (0,)), ((), ())), preferred_element_type=F32
        )
        for ex in range(EXM):
            block = outer[:, ex * r_dim : (ex + 1) * r_dim]
            psend[m, ex] = jnp.concatenate([block[:half], block[half:]], axis=1)
        for to, far, near in sketch_copies(m):

            @pl.when(to != me)
            def _():
                far.start()

            @pl.when(to == me)
            def _():
                near.start()

        return carry

    lax.fori_loop(0, n_micro, step, 0)
    lax.fori_loop(0, n_micro, outer_of, 0)

    @pl.when(first)
    def _():
        for m in range(n_micro):
            await_all(frecv[m], fr_sem.at[m])
            for t in range(tok_dev):
                total = combined(m, t, outgrad[m, t].astype(F32), frecv[m], 1)
                grads_ref[m, t] = total.astype(BF16)

    @pl.when(jnp.logical_not(first))
    def _():
        for m in range(n_micro):
            await_all(back.at[m], br_sem.at[m])
        grads_ref[...] = back[...]

    await_all(srecv, sr_sem)
    for q in range(q_dev):
        total = srecv[q, 0]
        for j in range(1, hsplit):
            total = total + srecv[q, j]
        sketch_ref[q] = total

    others = (n_expert - 1) * CAP
    await_all(metar.at[pl.ds(0, (n_expert - 1) * 16)], ms_sem)
    for m in range(n_micro):
        await_all(xrecv.at[m, pl.ds(0, others)], xs_sem.at[m])
        await_all(grecv.at[m, pl.ds(0, others)], gs_sem.at[m])

        @pl.when(first)
        def _():
            await_all(osend.at[m, pl.ds(0, others)], os_sem.at[m])

        @pl.when(jnp.logical_not(first))
        def _():
            await_all(osend.at[m], os_sem.at[m])
            await_all(outgrad.at[m], rs_sem.at[m])

        @pl.when(jnp.logical_not(last))
        def _():
            await_all(outgrad.at[m], bs_sem.at[m])

        for to, far, near in sketch_copies(m):

            @pl.when(to != me)
            def _():
                far.wait_send()


def on_device(
    saved_inputs,
    top_grad,
    expert_ids,
    route_weights,
    example_ids,
    gate_weight,
    up_weight,
    down_weight,
    left_proj,
    right_proj,
):
    n_section = lax.axis_size("section")
    n_expert = lax.axis_size("expert")
    groups = EXPERTS
    hsplit = n_expert // groups
    n_micro, tok_dev, feat = saved_inputs.shape[1:]
    top_k = expert_ids.shape[3]
    n_pairs = tok_dev * top_k
    n_slots = groups * CAP
    dk = feat // LANES
    hid = gate_weight.shape[1]
    r_dim = left_proj.shape[2]
    q_dev = n_micro * EXM * groups // n_expert

    ids = expert_ids[0].swapaxes(1, 2).reshape(n_micro, n_pairs)
    weights = route_weights[0].swapaxes(1, 2).reshape(n_micro, n_pairs).astype(F32)
    pair = jnp.arange(n_pairs, dtype=jnp.int32)
    same = (ids[:, :, None] == ids[:, None, :]) & (pair[:, None] > pair[None, :])[None]
    position = jnp.sum(same.astype(jnp.int32), axis=2)
    slot_of = ids * CAP + position
    row_of = ids * (hsplit * CAP) + position
    slots = jnp.arange(n_slots, dtype=jnp.int32)
    select = slot_of[:, None, :] == slots[None, :, None]
    tok_of_slot = jnp.sum(jnp.where(select, (pair % tok_dev)[None, None], 0), axis=2)
    slot_weight = jnp.sum(jnp.where(select, weights[:, None, :], 0.0), axis=2)
    example_pairs = jnp.concatenate([example_ids] * top_k, axis=1)
    slot_example = jnp.sum(jnp.where(select, example_pairs[:, None, :], 0), axis=2)
    lane_example = jnp.arange(EXM * r_dim, dtype=jnp.int32) // r_dim
    meta = jnp.where(
        slot_example[:, :, None] == lane_example[None, None], slot_weight[:, :, None], 0.0
    )
    meta = meta.reshape(n_micro, groups, CAP, EXM * r_dim).swapaxes(0, 1)
    meta = jnp.pad(meta, ((0, 0), (0, 0), (0, 4 - CAP), (0, 0)))
    meta = meta.reshape(groups, n_micro * 4, 2, LANES).swapaxes(1, 2)
    meta = meta.reshape(groups * 2 * n_micro * 4, LANES).astype(BF16)
    row_flat = row_of.reshape(n_micro * n_pairs)
    above = lax.ppermute(row_flat, "section", [(i, i - 1) for i in range(1, n_section)])
    row_table = jnp.concatenate([above, row_flat])

    n_rows = n_expert * CAP
    vmem = pl.BlockSpec(memory_space=pltpu.VMEM)
    smem = pl.BlockSpec(memory_space=pltpu.SMEM)
    hbm = pl.BlockSpec(memory_space=pl.ANY)
    dma = pltpu.SemaphoreType.DMA
    grads, sketch = pl.pallas_call(
        functools.partial(kernel, n_section, n_expert, groups),
        out_shape=(
            jax.ShapeDtypeStruct((n_micro, tok_dev, dk, LANES), BF16),
            jax.ShapeDtypeStruct((q_dev, r_dim // 2, 2 * r_dim), F32),
        ),
        in_specs=[smem, smem, vmem, vmem, vmem, vmem, hbm, hbm, hbm, hbm],
        out_specs=(vmem, vmem),
        scratch_shapes=[
            pltpu.VMEM((2 * hid, feat), BF16),
            pltpu.VMEM((hid + r_dim, feat), BF16),
            pltpu.VMEM((n_micro * tok_dev, dk, LANES), BF16),
            pltpu.VMEM((n_micro, n_slots, dk, LANES), BF16),
            pltpu.VMEM((n_micro, n_rows, dk, LANES), BF16),
            pltpu.VMEM((n_micro, n_slots, dk, LANES), BF16),
            pltpu.VMEM((n_micro, n_rows, dk, LANES), BF16),
            pltpu.VMEM((n_micro, n_rows, dk, LANES), BF16),
            pltpu.VMEM((n_rows, dk, LANES), BF16),
            pltpu.VMEM((n_rows, dk, LANES), BF16),
            pltpu.VMEM((n_rows, dk, LANES), BF16),
            pltpu.VMEM((n_rows, dk, LANES), BF16),
            pltpu.VMEM((n_expert * 16, LANES), BF16),
            pltpu.VMEM((n_expert * 16, LANES), F32),
            pltpu.VMEM((n_micro, tok_dev, dk, LANES), BF16),
            pltpu.VMEM((n_micro, tok_dev, dk, LANES), BF16),
            pltpu.VMEM((n_micro, tok_dev, dk, LANES), BF16),
            pltpu.VMEM((n_rows * dk, LANES), F32),
            pltpu.VMEM((n_rows, feat), BF16),
            pltpu.VMEM((n_rows, 2 * hid), BF16),
            pltpu.VMEM((n_micro, n_rows, hid), F32),
            pltpu.VMEM((n_micro, n_rows, hid), F32),
            pltpu.VMEM((n_micro, n_rows, r_dim), F32),
            pltpu.VMEM((n_micro, n_rows, r_dim), F32),
            pltpu.VMEM((n_micro, EXM, r_dim // 2, 2 * r_dim), F32),
            pltpu.VMEM((q_dev, hsplit, r_dim // 2, 2 * r_dim), F32),
            dma((4,)),
            dma((n_micro,)),
            dma((n_micro,)),
            dma((n_micro,)),
            dma((n_micro,)),
            dma((n_micro,)),
            dma((n_micro,)),
            dma((n_micro,)),
            dma(()),
            dma(()),
            dma((n_micro,)),
            dma((n_micro,)),
            dma((n_micro,)),
            dma((n_micro,)),
            dma((n_micro, EXM)),
            dma(()),
        ],
        compiler_params=pltpu.CompilerParams(collective_id=0, has_side_effects=True),
    )(
        tok_of_slot.reshape(n_micro * n_slots),
        row_table,
        saved_inputs.reshape(n_micro * tok_dev, feat),
        top_grad.reshape(n_micro * tok_dev, feat),
        meta,
        left_proj[0].T,
        gate_weight[0],
        up_weight[0],
        down_weight[0],
        right_proj[0].T,
    )
    return (
        grads.reshape(1, n_micro, tok_dev, feat),
        sketch.reshape(1, q_dev, r_dim * r_dim),
    )


def solution(mesh):
    placed = (
        P("section", None, "expert", None),
        P(None, "expert", None),
        P("section", None, "expert", None),
        P("section", None, "expert", None),
        P(None, "expert"),
        P("section", "expert", None),
        P("section", "expert", None),
        P("section", "expert", None),
        P("section", "expert", None),
        P("section", None, None),
    )
    return jax.shard_map(
        on_device,
        mesh=mesh,
        in_specs=placed,
        out_specs=(P("section", None, "expert", None), P("section", "expert", None)),
        check_vma=False,
    )
```

```python
import functools

import jax
import jax.numpy as jnp
from jax import lax
from jax.experimental import pallas as pl
from jax.experimental.pallas import tpu as pltpu
from jax.sharding import PartitionSpec as P

EXPERTS = 8
EXM = 4
CAP = 3
RING = 8
LANES = 128
F32 = jnp.float32
BF16 = jnp.bfloat16
MESH = pl.DeviceIdType.MESH


def far_first(n, me, n_expert):
    ring = RING if n_expert % RING == 0 else n_expert
    across = n_expert // ring

    def offset(rank, size):
        return size // 2 + (1 - 2 * lax.rem(rank, 2)) * ((rank + 1) // 2)

    z = lax.rem(lax.rem(me, ring) + offset(lax.rem(n, ring), ring), ring)
    x = lax.rem(me // ring + offset(n // ring, across), across)
    return x * ring + z


def kernel(
    n_section,
    n_expert,
    groups,
    tok_ref,
    row_ref,
    x_ref,
    top_ref,
    meta_ref,
    left_ref,
    gate_hbm,
    up_hbm,
    down_hbm,
    right_hbm,
    grads_ref,
    sketch_ref,
    wgu,
    wdr,
    xrows,
    xsend,
    xrecv,
    gsend,
    grecv,
    osend,
    crecv_a,
    crecv_b,
    frecv_a,
    frecv_b,
    metar,
    metaw,
    outgrad,
    resid,
    back,
    wide,
    rows,
    gcat,
    coef_g,
    coef_u,
    left_keep,
    right_keep,
    psend,
    srecv,
    w_sem,
    xs_sem,
    xr_sem,
    gs_sem,
    gr_sem,
    os_sem,
    cr_sem,
    fr_sem,
    ms_sem,
    mr_sem,
    rs_sem,
    rr_sem,
    bs_sem,
    br_sem,
    ss_sem,
    sr_sem,
):
    crecv, frecv = (crecv_a, crecv_b), (frecv_a, frecv_b)
    sec = lax.axis_index("section")
    me = lax.axis_index("expert")
    hsplit = n_expert // groups
    n_micro, tok_dev, dk, _ = outgrad.shape
    n_slots = groups * CAP
    hid = down_hbm.shape[0]
    top_k = row_ref.shape[0] // (2 * n_micro * tok_dev)
    q_dev = n_micro * EXM * groups // n_expert
    r_dim = left_ref.shape[0]
    half = r_dim // 2
    last = sec == n_section - 1
    first = sec == 0

    loads = [
        pltpu.make_async_copy(gate_hbm, wgu.at[pl.ds(0, hid)], w_sem.at[0]),
        pltpu.make_async_copy(up_hbm, wgu.at[pl.ds(hid, hid)], w_sem.at[1]),
        pltpu.make_async_copy(down_hbm, wdr.at[pl.ds(0, hid)], w_sem.at[2]),
        pltpu.make_async_copy(right_hbm, wdr.at[pl.ds(hid, r_dim)], w_sem.at[3]),
    ]
    for load in loads:
        load.start()

    barrier = pltpu.get_barrier_semaphore()

    def greet(other, skip_me):
        def one(n, carry):
            to = lax.rem(me + 1 + n, n_expert)
            pl.semaphore_signal(
                barrier, inc=1, device_id={"section": other, "expert": to}, device_id_type=MESH
            )
            return carry

        lax.fori_loop(0, n_expert - 1 if skip_me else n_expert, one, 0)

    greet(sec, True)

    @pl.when(jnp.logical_not(first))
    def _():
        greet(sec - 1, False)

    @pl.when(jnp.logical_not(last))
    def _():
        greet(sec + 1, False)

    def tiles_of(ref):
        n = n_micro * tok_dev
        for k in range(dk):
            wide[pl.ds(k, n, stride=dk), :] = ref[:, pl.ds(k * LANES, LANES)].astype(F32)
        return wide[pl.ds(0, n * dk), :].astype(BF16).reshape(n, dk, LANES)

    xrows[...] = tiles_of(x_ref)

    @pl.when(last)
    def _():
        outgrad[...] = tiles_of(top_ref).reshape(n_micro, tok_dev, dk, LANES)

    def xbuild(m, carry):
        for s in range(n_slots):
            xsend[m, s] = xrows[m * tok_dev + tok_ref[m * n_slots + s]]
        return carry

    lax.fori_loop(0, n_micro, xbuild, 0)

    met = (
        n_expert - 1
        + jnp.where(first, 0, n_expert)
        + jnp.where(last, 0, n_expert)
    )
    pl.semaphore_wait(barrier, met)

    def spread(src, per, dst, send_sem, recv_sem):
        def one(n, carry):
            to = far_first(n, me, n_expert)
            pltpu.make_async_remote_copy(
                src_ref=src.at[pl.ds((to // hsplit) * per, per)],
                dst_ref=dst.at[pl.ds(me * per, per)],
                send_sem=send_sem,
                recv_sem=recv_sem,
                device_id={"section": sec, "expert": to},
                device_id_type=MESH,
            ).start()
            return carry

        for n in range(n_expert - 1):
            one(n, 0)
        pltpu.make_async_copy(
            src.at[pl.ds((me // hsplit) * per, per)], dst.at[pl.ds(me * per, per)], recv_sem
        ).start()

    def await_all(ref, sem):
        pltpu.make_async_copy(ref, ref, sem).wait()

    def dispatch(m):
        for s in range(n_slots):
            gsend[m, s] = outgrad[m, tok_ref[m * n_slots + s]]
        spread(gsend.at[m], CAP, grecv.at[m], gs_sem.at[m], gr_sem.at[m])

        @pl.when(jnp.logical_not(first))
        def _():
            pltpu.make_async_remote_copy(
                src_ref=outgrad.at[m],
                dst_ref=resid.at[m],
                send_sem=rs_sem.at[m],
                recv_sem=rr_sem.at[m],
                device_id={"section": sec - 1, "expert": me},
                device_id_type=MESH,
            ).start()

        @pl.when(jnp.logical_not(last))
        def _():
            pltpu.make_async_remote_copy(
                src_ref=outgrad.at[m],
                dst_ref=back.at[m],
                send_sem=bs_sem.at[m],
                recv_sem=br_sem.at[m],
                device_id={"section": sec + 1, "expert": me},
                device_id_type=MESH,
            ).start()

    def combined(m, t, base, parts, which):
        total = base
        for k in range(top_k):
            at = row_ref[((which * n_micro + m) * top_k + k) * tok_dev + t]
            for j in range(hsplit):
                total = total + parts[at + j * CAP].astype(F32)
        return total

    def send_inputs(m):
        spread(xsend.at[m], CAP, xrecv.at[m], xs_sem.at[m], xr_sem.at[m])

    send_inputs(0)
    spread(meta_ref, 16, metar, ms_sem, mr_sem)

    @pl.when(last)
    def _():
        def start_micro(m, carry):
            @pl.when(m > 0)
            def _():
                send_inputs(m)

            dispatch(m)
            return carry

        lax.fori_loop(0, n_micro, start_micro, 0)

    def by_row(ref, m):
        wide[...] = ref[m].reshape(n_expert * CAP * dk, LANES).astype(F32)
        for k in range(dk):
            for c in range(CAP):
                rows[pl.ds(c * n_expert, n_expert), pl.ds(k * LANES, LANES)] = wide[
                    pl.ds(c * dk + k, n_expert, stride=CAP * dk), :
                ].astype(BF16)

    def meta_of(m):
        return jnp.concatenate(
            [
                jnp.concatenate(
                    [metaw[pl.ds(b * 8 + m * 4 + c, n_expert, stride=16), :] for b in range(2)],
                    axis=1,
                )
                for c in range(CAP)
            ],
            axis=0,
        )

    contract_last = (((1,), (1,)), ((), ()))
    for load in loads:
        load.wait()
    await_all(metar, mr_sem)
    metaw[...] = metar[...].astype(F32)

    def forward(m, carry):
        await_all(xrecv.at[m], xr_sem.at[m])
        by_row(xrecv, m)
        both = lax.dot_general(rows[...], wgu[...], contract_last, preferred_element_type=F32)
        pre_gate, pre_up = both[:, :hid], both[:, hid:]
        sigmoid_g = jax.nn.sigmoid(pre_gate)
        silu = pre_gate * sigmoid_g
        hidden = (silu * pre_up).astype(BF16)
        left_keep[m] = lax.dot_general(
            hidden, left_ref[...], contract_last, preferred_element_type=F32
        )
        weight = jnp.max(meta_of(m), axis=1, keepdims=True)
        coef_g[m] = weight * (pre_up * sigmoid_g * (1.0 + pre_gate * (1.0 - sigmoid_g)))
        coef_u[m] = weight * silu
        return carry

    @pl.when(jnp.logical_not(last))
    def _():
        def prepare(m, carry):
            forward(m, 0)

            @pl.when(m + 1 < n_micro)
            def _():
                send_inputs(m + 1)

            return carry

        lax.fori_loop(0, n_micro, prepare, 0)

    def to_homes(m, other, skip_me, dst, recv_sem):
        def one(n, carry):
            to = far_first(n, me, n_expert)
            pltpu.make_async_remote_copy(
                src_ref=osend.at[m, pl.ds(to * CAP, CAP)],
                dst_ref=dst.at[pl.ds(me * CAP, CAP)],
                send_sem=os_sem.at[m],
                recv_sem=recv_sem,
                device_id={"section": other, "expert": to},
                device_id_type=MESH,
            ).start()
            return carry

        for n in range(n_expert - 1 if skip_me else n_expert):
            one(n, 0)

    def sketch_copies(m):
        mine = me // hsplit
        copies = []
        for ex in range(EXM):
            q = (m * EXM + ex) * groups + mine
            to = q // q_dev
            src = psend.at[m, ex]
            dst = srecv.at[lax.rem(q, q_dev), lax.rem(me, hsplit)]
            far = pltpu.make_async_remote_copy(
                src_ref=src,
                dst_ref=dst,
                send_sem=ss_sem.at[m, ex],
                recv_sem=sr_sem,
                device_id={"section": sec, "expert": to},
                device_id_type=MESH,
            )
            near = pltpu.make_async_copy(src, dst, sr_sem)
            copies.append((to, far, near))
        return copies

    def home(m, carry):
        await_all(resid.at[m], rr_sem.at[m])
        for which in range(n_micro):

            @pl.when(m == which)
            def _():
                await_all(crecv[which], cr_sem.at[which])
                for t in range(tok_dev):
                    base = resid[which, t].astype(F32)
                    total = combined(which, t, base, crecv[which], 0)
                    outgrad[which, t] = total.astype(BF16)

        dispatch(m)
        return carry

    @pl.when(jnp.logical_not(last))
    def _():
        lax.fori_loop(0, n_micro, home, 0)

    def step(m, carry):
        @pl.when(last)
        def _():
            forward(m, 0)

        await_all(grecv.at[m], gr_sem.at[m])
        by_row(grecv, m)
        both = lax.dot_general(
            rows[...], wdr[...], contract_last, preferred_element_type=F32
        )
        grad_hidden, right = both[:, :hid], both[:, hid:]
        gcat[:, pl.ds(0, hid)] = (grad_hidden * coef_g[m]).astype(BF16)
        gcat[:, pl.ds(hid, hid)] = (grad_hidden * coef_u[m]).astype(BF16)
        for n in range(dk // 2):
            part = jnp.dot(
                gcat[...], wgu[:, pl.ds(n * 2 * LANES, 2 * LANES)], preferred_element_type=F32
            )
            for b in range(2):
                k = n * 2 + b
                for c in range(CAP):
                    wide[pl.ds(c * dk + k, n_expert, stride=CAP * dk), :] = part[
                        c * n_expert : (c + 1) * n_expert, b * LANES : (b + 1) * LANES
                    ]
        osend[m] = wide[...].astype(BF16).reshape(n_expert * CAP, dk, LANES)

        for which in range(n_micro):

            @pl.when((m == which) & first)
            def _():
                to_homes(which, sec, True, frecv[which], fr_sem.at[which])
                pltpu.make_async_copy(
                    osend.at[which, pl.ds(me * CAP, CAP)],
                    frecv[which].at[pl.ds(me * CAP, CAP)],
                    fr_sem.at[which],
                ).start()

            @pl.when((m == which) & jnp.logical_not(first))
            def _():
                to_homes(which, sec - 1, False, crecv[which], cr_sem.at[which])

        right_keep[m] = right
        return carry

    def outer_of(m, carry):
        right = jnp.concatenate([right_keep[m]] * EXM, axis=1) * meta_of(m)
        left = left_keep[m].astype(BF16)
        at_r = lax.broadcasted_iota(jnp.int32, (r_dim, r_dim), 0)
        at_c = lax.broadcasted_iota(jnp.int32, (r_dim, r_dim), 1)
        place = lax.rem(at_r, 2) * half + lax.div(at_r, 2)
        shuffle = jnp.where(at_c == place, 1.0, 0.0).astype(BF16)
        left = jnp.dot(left, shuffle, preferred_element_type=F32).astype(BF16)
        outer = lax.dot_general(
            left, right.astype(BF16), (((0,), (0,)), ((), ())), preferred_element_type=F32
        )
        for ex in range(EXM):
            block = outer[:, ex * r_dim : (ex + 1) * r_dim]
            psend[m, ex] = jnp.concatenate([block[:half], block[half:]], axis=1)
        for to, far, near in sketch_copies(m):

            @pl.when(to != me)
            def _():
                far.start()

            @pl.when(to == me)
            def _():
                near.start()

        return carry

    lax.fori_loop(0, n_micro, step, 0)
    lax.fori_loop(0, n_micro, outer_of, 0)

    @pl.when(first)
    def _():
        for m in range(n_micro):
            await_all(frecv[m], fr_sem.at[m])
            for t in range(tok_dev):
                total = combined(m, t, outgrad[m, t].astype(F32), frecv[m], 1)
                grads_ref[m, t] = total.astype(BF16)

    @pl.when(jnp.logical_not(first))
    def _():
        for m in range(n_micro):
            await_all(back.at[m], br_sem.at[m])
        grads_ref[...] = back[...]

    await_all(srecv, sr_sem)
    for q in range(q_dev):
        total = srecv[q, 0]
        for j in range(1, hsplit):
            total = total + srecv[q, j]
        sketch_ref[q] = total

    others = (n_expert - 1) * CAP
    await_all(metar.at[pl.ds(0, (n_expert - 1) * 16)], ms_sem)
    for m in range(n_micro):
        await_all(xrecv.at[m, pl.ds(0, others)], xs_sem.at[m])
        await_all(grecv.at[m, pl.ds(0, others)], gs_sem.at[m])

        @pl.when(first)
        def _():
            await_all(osend.at[m, pl.ds(0, others)], os_sem.at[m])

        @pl.when(jnp.logical_not(first))
        def _():
            await_all(osend.at[m], os_sem.at[m])
            await_all(outgrad.at[m], rs_sem.at[m])

        @pl.when(jnp.logical_not(last))
        def _():
            await_all(outgrad.at[m], bs_sem.at[m])

        for to, far, near in sketch_copies(m):

            @pl.when(to != me)
            def _():
                far.wait_send()


def on_device(
    saved_inputs,
    top_grad,
    expert_ids,
    route_weights,
    example_ids,
    gate_weight,
    up_weight,
    down_weight,
    left_proj,
    right_proj,
):
    n_section = lax.axis_size("section")
    n_expert = lax.axis_size("expert")
    groups = EXPERTS
    hsplit = n_expert // groups
    n_micro, tok_dev, feat = saved_inputs.shape[1:]
    top_k = expert_ids.shape[3]
    n_pairs = tok_dev * top_k
    n_slots = groups * CAP
    dk = feat // LANES
    hid = gate_weight.shape[1]
    r_dim = left_proj.shape[2]
    q_dev = n_micro * EXM * groups // n_expert

    ids = expert_ids[0].swapaxes(1, 2).reshape(n_micro, n_pairs)
    weights = route_weights[0].swapaxes(1, 2).reshape(n_micro, n_pairs).astype(F32)
    pair = jnp.arange(n_pairs, dtype=jnp.int32)
    same = (ids[:, :, None] == ids[:, None, :]) & (pair[:, None] > pair[None, :])[None]
    position = jnp.sum(same.astype(jnp.int32), axis=2)
    slot_of = ids * CAP + position
    row_of = ids * (hsplit * CAP) + position
    slots = jnp.arange(n_slots, dtype=jnp.int32)
    select = slot_of[:, None, :] == slots[None, :, None]
    tok_of_slot = jnp.sum(jnp.where(select, (pair % tok_dev)[None, None], 0), axis=2)
    slot_weight = jnp.sum(jnp.where(select, weights[:, None, :], 0.0), axis=2)
    example_pairs = jnp.concatenate([example_ids] * top_k, axis=1)
    slot_example = jnp.sum(jnp.where(select, example_pairs[:, None, :], 0), axis=2)
    lane_example = jnp.arange(EXM * r_dim, dtype=jnp.int32) // r_dim
    meta = jnp.where(
        slot_example[:, :, None] == lane_example[None, None], slot_weight[:, :, None], 0.0
    )
    meta = meta.reshape(n_micro, groups, CAP, EXM * r_dim).swapaxes(0, 1)
    meta = jnp.pad(meta, ((0, 0), (0, 0), (0, 4 - CAP), (0, 0)))
    meta = meta.reshape(groups, n_micro * 4, 2, LANES).swapaxes(1, 2)
    meta = meta.reshape(groups * 2 * n_micro * 4, LANES).astype(BF16)
    row_flat = row_of.reshape(n_micro * n_pairs)
    above = lax.ppermute(row_flat, "section", [(i, i - 1) for i in range(1, n_section)])
    row_table = jnp.concatenate([above, row_flat])

    n_rows = n_expert * CAP
    vmem = pl.BlockSpec(memory_space=pltpu.VMEM)
    smem = pl.BlockSpec(memory_space=pltpu.SMEM)
    hbm = pl.BlockSpec(memory_space=pl.ANY)
    dma = pltpu.SemaphoreType.DMA
    grads, sketch = pl.pallas_call(
        functools.partial(kernel, n_section, n_expert, groups),
        out_shape=(
            jax.ShapeDtypeStruct((n_micro, tok_dev, dk, LANES), BF16),
            jax.ShapeDtypeStruct((q_dev, r_dim // 2, 2 * r_dim), F32),
        ),
        in_specs=[smem, smem, vmem, vmem, vmem, vmem, hbm, hbm, hbm, hbm],
        out_specs=(vmem, vmem),
        scratch_shapes=[
            pltpu.VMEM((2 * hid, feat), BF16),
            pltpu.VMEM((hid + r_dim, feat), BF16),
            pltpu.VMEM((n_micro * tok_dev, dk, LANES), BF16),
            pltpu.VMEM((n_micro, n_slots, dk, LANES), BF16),
            pltpu.VMEM((n_micro, n_rows, dk, LANES), BF16),
            pltpu.VMEM((n_micro, n_slots, dk, LANES), BF16),
            pltpu.VMEM((n_micro, n_rows, dk, LANES), BF16),
            pltpu.VMEM((n_micro, n_rows, dk, LANES), BF16),
            pltpu.VMEM((n_rows, dk, LANES), BF16),
            pltpu.VMEM((n_rows, dk, LANES), BF16),
            pltpu.VMEM((n_rows, dk, LANES), BF16),
            pltpu.VMEM((n_rows, dk, LANES), BF16),
            pltpu.VMEM((n_expert * 16, LANES), BF16),
            pltpu.VMEM((n_expert * 16, LANES), F32),
            pltpu.VMEM((n_micro, tok_dev, dk, LANES), BF16),
            pltpu.VMEM((n_micro, tok_dev, dk, LANES), BF16),
            pltpu.VMEM((n_micro, tok_dev, dk, LANES), BF16),
            pltpu.VMEM((n_rows * dk, LANES), F32),
            pltpu.VMEM((n_rows, feat), BF16),
            pltpu.VMEM((n_rows, 2 * hid), BF16),
            pltpu.VMEM((n_micro, n_rows, hid), F32),
            pltpu.VMEM((n_micro, n_rows, hid), F32),
            pltpu.VMEM((n_micro, n_rows, r_dim), F32),
            pltpu.VMEM((n_micro, n_rows, r_dim), F32),
            pltpu.VMEM((n_micro, EXM, r_dim // 2, 2 * r_dim), F32),
            pltpu.VMEM((q_dev, hsplit, r_dim // 2, 2 * r_dim), F32),
            dma((4,)),
            dma((n_micro,)),
            dma((n_micro,)),
            dma((n_micro,)),
            dma((n_micro,)),
            dma((n_micro,)),
            dma((n_micro,)),
            dma((n_micro,)),
            dma(()),
            dma(()),
            dma((n_micro,)),
            dma((n_micro,)),
            dma((n_micro,)),
            dma((n_micro,)),
            dma((n_micro, EXM)),
            dma(()),
        ],
        compiler_params=pltpu.CompilerParams(collective_id=0, has_side_effects=True),
    )(
        tok_of_slot.reshape(n_micro * n_slots),
        row_table,
        saved_inputs.reshape(n_micro * tok_dev, feat),
        top_grad.reshape(n_micro * tok_dev, feat),
        meta,
        left_proj[0].T,
        gate_weight[0],
        up_weight[0],
        down_weight[0],
        right_proj[0].T,
    )
    return (
        grads.reshape(1, n_micro, tok_dev, feat),
        sketch.reshape(1, q_dev, r_dim * r_dim),
    )


def solution(mesh):
    placed = (
        P("section", None, "expert", None),
        P(None, "expert", None),
        P("section", None, "expert", None),
        P("section", None, "expert", None),
        P(None, "expert"),
        P("section", "expert", None),
        P("section", "expert", None),
        P("section", "expert", None),
        P("section", "expert", None),
        P("section", None, None),
    )
    return jax.shard_map(
        on_device,
        mesh=mesh,
        in_specs=placed,
        out_specs=(P("section", None, "expert", None), P("section", "expert", None)),
        check_vma=False,
    )
```
